128 devices in a mesh: freq: 8 (over x, core), space: 16 (over y, z).
Axes of the slice: x: 4, y: 4, z: 4, core: 2. Of those that a mesh axis runs over, the one named last changes fastest.
Arguments:
- traces: float32 [128, 128, 2048], P('space', 'freq'), may hold values from -6 to 6
- kept_bins: int32 [8], replicated, may hold values from 8 to 1015, as said below
- start_basis: float32 [8, 2, 40, 256], P('freq'), may hold values from -6 to 6
Outputs:
- denoised: float32 [128, 128, 2048], P('space', 'freq')
The draws below stay inside these ranges and needn't reach their ends.
Inputs may be any that keep to these rules, and one draw needn't show every extreme that they name: `kept_bins`: 8 distinct bins in rising order; the first is the band's lower limit and the last its upper limit.
All inputs are finite; a program needn't handle non-finite values.
Results may differ from the reference program's by a relative error of at most 0.00019.
Values sent between devices are 32-bit elements; how exact they have to be, the bound alone decides.
A program may use at most 128 MiB of HBM per device.

```python
import math
import jax
import jax.numpy as jnp
from jax import lax

NT = 2048
LX = 8
LY = 32
RANK = 40
POWER = 4
CADZOW = 2
NY = 128
NX = 128
NF = 8


def draw_kept_bins(key, part):
    inner = jax.random.permutation(key, NT // 2 - 18)[:NF - 2].astype(jnp.int32) + 9
    inner = jnp.sort(inner)
    lowest = jnp.array([8], jnp.int32)
    highest = jnp.array([NT // 2 - 9], jnp.int32)
    return jnp.concatenate([lowest, inner, highest])


def steps_of(stream_key, shape, cuts, least, high):
    loudness, own = 1.0, jax.random.fold_in(stream_key, 6)
    for position, shards_of in cuts:
        heights = jnp.exp(jax.random.uniform(jax.random.fold_in(own, position), (shards_of,), jnp.float32, least / len(cuts), high / len(cuts)))
        loudness = loudness * jnp.repeat(heights, shape[position] // shards_of).reshape([-1 if axis == position else 1 for axis in range(len(shape))])
    return loudness


def noise(rng, shape, width, reach, cuts=(), kind=jnp.bfloat16):
    drawn = width * jax.random.normal(rng, shape, jnp.float32)
    if cuts:
        drawn = drawn * steps_of(rng, shape, cuts, -0.22, 0.18)
    return jnp.clip(drawn, -reach, reach).astype(kind)


def setup_inputs(seed: int = 0) -> dict:
    seeds = jax.random.split(jax.random.key(seed), 4)
    traces = noise(seeds[0], (NX, NY, NT), 1.0, 6.0, ((0, 16), (1, 8)), jnp.float32)
    kept_bins = draw_kept_bins(jax.random.fold_in(seeds[3], 71), 0)
    start_basis = noise(seeds[2], (NF, 2, RANK, LX * LY), 1.0, 6.0, ((0, 8),), jnp.float32)
    return {"traces": traces, "kept_bins": kept_bins, "start_basis": start_basis}


exact_mode = lax.Precision.HIGHEST

def matmul(left, right):
    return jnp.dot(left.astype(jnp.float32), right.astype(jnp.float32), precision=exact_mode, preferred_element_type=jnp.float32)

def tables(kept_bins):
    samples = jnp.arange(NT, dtype=jnp.int32)
    phases = samples[:, None] * kept_bins[None, :] % NT
    angles = phases.astype(jnp.float32) * (2.0 * math.pi / NT)
    return (jnp.cos(angles), jnp.sin(angles))

def valid_columns():
    xpos = jnp.arange(NX, dtype=jnp.int32)
    ypos = jnp.arange(NY, dtype=jnp.int32)
    valid_cols = (xpos < NX - LX + 1)[:, None] & (ypos < NY - LY + 1)[None, :]
    return valid_cols.astype(jnp.float32).reshape(NX * NY)

def hankel(slices):
    padded = jnp.pad(slices, ((0, 0), (0, LX - 1), (0, LY - 1)))
    pieces = [padded[:, lag_x:lag_x + NX, lag_y:lag_y + NY] for lag_x in range(LX) for lag_y in range(LY)]
    matrix = jnp.stack(pieces, axis=1).reshape(2, LX * LY, NX * NY)
    return matrix * valid_columns()

def paired(start):
    real_rows = jnp.concatenate([start[0], -start[1]], axis=0)
    imag_rows = jnp.concatenate([start[1], start[0]], axis=0)
    return jnp.stack([real_rows, imag_rows])

def adjoint(matrix, subspace):
    real_part = matmul(subspace[0], matrix[0]) + matmul(subspace[1], matrix[1])
    imag_part = matmul(subspace[1], matrix[0]) - matmul(subspace[0], matrix[1])
    return jnp.stack([real_part, imag_part])

def forward(matrix, coeffs):
    real_part = matmul(coeffs[0], matrix[0].T) - matmul(coeffs[1], matrix[1].T)
    imag_part = matmul(coeffs[0], matrix[1].T) + matmul(coeffs[1], matrix[0].T)
    return jnp.stack([real_part, imag_part])

def orthonormal(product_rows):
    gram_matrix = matmul(product_rows[0], product_rows[0].T) + matmul(product_rows[1], product_rows[1].T)
    factor = jnp.linalg.cholesky(gram_matrix)
    flattened = jnp.concatenate([product_rows[0], product_rows[1]], axis=1)
    solved = lax.linalg.triangular_solve(factor, flattened, left_side=True, lower=True)
    return jnp.stack([solved[:, :LX * LY], solved[:, LX * LY:]])

def counts_along(length, lags, limit):
    places = jnp.arange(length, dtype=jnp.int32)
    total = jnp.zeros((length,), jnp.float32)
    for shift_by in range(lags):
        inside = (places - shift_by >= 0) & (places - shift_by < limit)
        total = total + inside.astype(jnp.float32)
    return total

def average(projected):
    blocks = projected.reshape(2, LX, LY, NX, NY)
    total = jnp.zeros((2, NX, NY), jnp.float32)
    for lag_x in range(LX):
        for lag_y in range(LY):
            moved = jnp.pad(blocks[:, lag_x, lag_y], ((0, 0), (lag_x, 0), (lag_y, 0)))
            total = total + moved[:, :NX, :NY]
    count_x = counts_along(NX, LX, NX - LX + 1)
    count_y = counts_along(NY, LY, NY - LY + 1)
    return total / (count_x[:, None] * count_y[None, :])

def cadzow(operands):
    slices, start = operands
    subspace = paired(start)
    for cadzow_step in range(CADZOW):
        matrix = hankel(slices)
        for power_step in range(POWER):
            subspace = orthonormal(forward(matrix, adjoint(matrix, subspace)))
        coeffs = adjoint(matrix, subspace)
        real_part = 0.5 * (matmul(subspace[0].T, coeffs[0]) + matmul(subspace[1].T, coeffs[1]))
        imag_part = 0.5 * (matmul(subspace[1].T, coeffs[0]) - matmul(subspace[0].T, coeffs[1]))
        slices = average(jnp.stack([real_part, imag_part]))
    return slices

def reference(traces, kept_bins, start_basis):
    cosines, sines = tables(kept_bins)
    dft_scale = 1.0 / math.sqrt(NT)
    real_part = jnp.einsum('xyt,tf->fxy', traces, cosines, precision=exact_mode) * dft_scale
    imag_part = -jnp.einsum('xyt,tf->fxy', traces, sines, precision=exact_mode) * dft_scale
    spectra = jnp.stack([real_part, imag_part], axis=1)
    cleaned = lax.map(cadzow, (spectra, start_basis))
    out_scale = math.sqrt(2.0 / NF)
    synth = jnp.einsum('fxy,tf->xyt', cleaned[:, 0], cosines, precision=exact_mode)
    synth = synth - jnp.einsum('fxy,tf->xyt', cleaned[:, 1], sines, precision=exact_mode)
    return out_scale * synth
```

```python
import math

import jax
import jax.numpy as jnp
from jax import lax
from jax.sharding import PartitionSpec as P

NT = 2048
LX = 8
LY = 32
RANK = 40
POWER = 4
CADZOW = 2


exact_mode = lax.Precision.HIGHEST


def shifted(x, axis, by):
    count = lax.axis_size(axis)
    pairs = [(i, i + by) for i in range(count) if 0 <= i + by < count]
    return lax.ppermute(x, axis, pairs)


def all_sum(x, axis):
    count = lax.axis_size(axis)
    chunks = x.reshape(count, -1)
    mine = lax.all_to_all(chunks, axis, 0, 0, tiled=True).sum(axis=0)
    copies = jnp.broadcast_to(mine[None], (count, mine.shape[0]))
    return lax.all_to_all(copies, axis, 0, 0, tiled=True).reshape(x.shape)


def product(form, left, right):
    return jnp.einsum(form, left, right, precision=exact_mode, preferred_element_type=jnp.float32)


def tables(kept_bins):
    samples = jnp.arange(NT, dtype=jnp.int32)
    phases = samples[:, None] * kept_bins[None, :] % NT
    angles = phases.astype(jnp.float32) * (2.0 * math.pi / NT)
    return (jnp.cos(angles), jnp.sin(angles))


def paired(start):
    real_rows = jnp.concatenate([start[:, 0], -start[:, 1]], axis=1)
    imag_rows = jnp.concatenate([start[:, 1], start[:, 0]], axis=1)
    return jnp.concatenate([real_rows, imag_rows], axis=2)


def shift_matrix(length, lags, limit):
    shape = (length, lags, length)
    z = lax.broadcasted_iota(jnp.int32, shape, 0)
    b = lax.broadcasted_iota(jnp.int32, shape, 1)
    y = lax.broadcasted_iota(jnp.int32, shape, 2)
    return ((z == y + b) & (y < limit)).astype(jnp.float32)


def realified(real_part, imag_part):
    top = jnp.concatenate([real_part, -imag_part], axis=-1)
    bottom = jnp.concatenate([imag_part, real_part], axis=-1)
    return jnp.concatenate([top, bottom], axis=-2)


def counts_along(places, lags, limit):
    total = jnp.zeros(places.shape, jnp.float32)
    for shift_by in range(lags):
        inside = (places - shift_by >= 0) & (places - shift_by < limit)
        total = total + inside.astype(jnp.float32)
    return total


def on_device(traces, kept_bins, start_basis):
    space_count = lax.axis_size("space")
    cosines, sines = tables(kept_bins)
    dft_scale = 1.0 / math.sqrt(NT)
    real_part = product("xyt,tf->fxy", traces, cosines) * dft_scale
    imag_part = -product("xyt,tf->fxy", traces, sines) * dft_scale
    spectra_tile = jnp.stack([real_part, imag_part], axis=1)
    slices = lax.all_to_all(spectra_tile, "freq", split_axis=0, concat_axis=3, tiled=True)
    freq_count = slices.shape[0]
    strip_width = slices.shape[2]
    trace_cols = slices.shape[3]
    rows = LX * LY
    x_offset = lax.axis_index("space") * strip_width
    places = x_offset + jnp.arange(strip_width, dtype=jnp.int32)
    columns = jnp.arange(trace_cols, dtype=jnp.int32)
    limit_x = strip_width * space_count - LX + 1
    limit_y = trace_cols - LY + 1
    valid_x = (places < limit_x).astype(jnp.float32)
    counts = (
        counts_along(places, LX, limit_x)[:, None] * counts_along(columns, LY, limit_y)[None, :]
    )
    lag_shift = shift_matrix(trace_cols, LY, limit_y)
    subspace = paired(start_basis)
    for cadzow_step in range(CADZOW):
        rim_rows = shifted(slices[:, :, : LX - 1, :], "space", -1)
        extended = jnp.concatenate([slices, rim_rows], axis=2)
        lagged = product("fcpz,zby->fcbpy", extended, lag_shift)
        matrix = jnp.stack(
            [lagged[:, :, :, lag_x : lag_x + strip_width, :] for lag_x in range(LX)], axis=2
        )
        matrix = matrix * valid_x[:, None]
        matrix = matrix.reshape(freq_count, 2 * rows, strip_width * trace_cols)
        gram_h = product("fik,fjk->fij", matrix, matrix)
        cov_real = gram_h[:, :rows, :rows] + gram_h[:, rows:, rows:]
        cov_imag = gram_h[:, rows:, :rows] - gram_h[:, :rows, rows:]
        cov = all_sum(jnp.stack([cov_real, cov_imag], axis=1), "space")
        cov_block = realified(cov[:, 0], cov[:, 1])
        for power_step in range(POWER):
            summed = product("fjk,fkl->fjl", subspace, cov_block)
            gram_matrix = product("fjk,fik->fji", summed, summed)
            factor = jnp.linalg.cholesky(gram_matrix)
            subspace = lax.linalg.triangular_solve(factor, summed, left_side=True, lower=True)
        gram_q = product("fjk,fjl->fkl", subspace, subspace)
        proj_real = 0.5 * (gram_q[:, :rows, :rows] + gram_q[:, rows:, rows:])
        proj_imag = 0.5 * (gram_q[:, rows:, :rows] - gram_q[:, :rows, rows:])
        projected = product("fij,fjk->fik", realified(proj_real, proj_imag), matrix)
        projected = projected.reshape(freq_count, 2, LX, LY, strip_width, trace_cols)
        along_y = product("fcabxy,vby->fcaxv", projected, lag_shift)
        full = sum(
            jnp.pad(along_y[:, :, lag_x], ((0, 0), (0, 0), (lag_x, LX - 1 - lag_x), (0, 0)))
            for lag_x in range(LX)
        )
        spill = shifted(full[:, :, strip_width:, :], "space", 1)
        spill = jnp.pad(spill, ((0, 0), (0, 0), (0, strip_width - (LX - 1)), (0, 0)))
        slices = (full[:, :, :strip_width, :] + spill) / counts
    out_scale = math.sqrt(2.0 / kept_bins.shape[0])
    received = lax.all_to_all(slices, "freq", split_axis=3, concat_axis=0, tiled=True)
    synth = product("fxy,tf->xyt", received[:, 0], cosines)
    synth = synth - product("fxy,tf->xyt", received[:, 1], sines)
    return out_scale * synth


def solution(mesh):
    placed = (P("space", "freq", None), P(), P("freq", None, None, None))
    return jax.shard_map(
        on_device, mesh=mesh, in_specs=placed, out_specs=P("space", "freq", None), check_vma=False
    )
```

```python
import math

import jax
import jax.numpy as jnp
from jax import lax
from jax.experimental import pallas as pl
from jax.sharding import PartitionSpec as P

NT = 2048
LX = 8
LY = 32
RANK = 40
POWER = 4
CADZOW = 2


exact_mode = lax.Precision.HIGHEST


def shifted(x, axis, by):
    count = lax.axis_size(axis)
    pairs = [(i, i + by) for i in range(count) if 0 <= i + by < count]
    return lax.ppermute(x, axis, pairs)


def all_sum(x, axis):
    count = lax.axis_size(axis)
    chunks = x.reshape(count, -1)
    mine = lax.all_to_all(chunks, axis, 0, 0, tiled=True).sum(axis=0)
    copies = jnp.broadcast_to(mine[None], (count, mine.shape[0]))
    return lax.all_to_all(copies, axis, 0, 0, tiled=True).reshape(x.shape)


def product(form, left, right):
    return jnp.einsum(form, left, right, precision=exact_mode, preferred_element_type=jnp.float32)


def tables(kept_bins):
    samples = jnp.arange(NT, dtype=jnp.int32)
    phases = samples[:, None] * kept_bins[None, :] % NT
    angles = phases.astype(jnp.float32) * (2.0 * math.pi / NT)
    return (jnp.cos(angles), jnp.sin(angles))


def paired(start):
    real_rows = jnp.concatenate([start[:, 0], -start[:, 1]], axis=1)
    imag_rows = jnp.concatenate([start[:, 1], start[:, 0]], axis=1)
    return jnp.concatenate([real_rows, imag_rows], axis=2)


def shift_matrix(length, lags, limit):
    shape = (length, lags, length)
    z = lax.broadcasted_iota(jnp.int32, shape, 0)
    b = lax.broadcasted_iota(jnp.int32, shape, 1)
    y = lax.broadcasted_iota(jnp.int32, shape, 2)
    return ((z == y + b) & (y < limit)).astype(jnp.float32)


def realified(real_part, imag_part):
    top = jnp.concatenate([real_part, -imag_part], axis=-1)
    bottom = jnp.concatenate([imag_part, real_part], axis=-1)
    return jnp.concatenate([top, bottom], axis=-2)


def inverse_factor(gram):
    count = gram.shape[0]
    row_id = lax.broadcasted_iota(jnp.int32, gram.shape, 0)
    col_id = lax.broadcasted_iota(jnp.int32, gram.shape, 1)
    eye = (row_id == col_id).astype(jnp.float32)

    def body(k, carry):
        left, inverse, pivots = carry
        at_row = row_id == k
        col_left = jnp.sum(jnp.where(col_id == k, left, 0.0), axis=1, keepdims=True)
        row_left = jnp.sum(jnp.where(at_row, left, 0.0), axis=0, keepdims=True)
        row_inverse = jnp.sum(jnp.where(at_row, inverse, 0.0), axis=0, keepdims=True)
        pivot = jnp.sum(jnp.where(at_row[:, :1], col_left, 0.0), axis=0, keepdims=True)
        below = jnp.where(row_id[:, :1] > k, col_left, 0.0) * (1.0 / pivot)
        left = left - below * row_left
        inverse = inverse - below * row_inverse
        pivots = jnp.where(row_id[:, :1] == k, pivot, pivots)
        return left, inverse, pivots

    start = (gram, eye, jnp.zeros((count, 1), jnp.float32))
    _, inverse, pivots = lax.fori_loop(0, count, body, start)
    return inverse * lax.rsqrt(pivots)


def power_kernel(cov_ref, start_ref, out_ref):
    cov = cov_ref[0]
    subspace = start_ref[0]
    for power_step in range(POWER):
        summed = jnp.dot(subspace, cov, precision=exact_mode, preferred_element_type=jnp.float32)
        gram_matrix = lax.dot_general(
            summed, summed, (((1,), (1,)), ((), ())), precision=exact_mode,
            preferred_element_type=jnp.float32,
        )
        subspace = jnp.dot(
            inverse_factor(gram_matrix), summed, precision=exact_mode,
            preferred_element_type=jnp.float32,
        )
    out_ref[0] = subspace


def power_steps(cov_block, subspace):
    freq_count, basis, width = subspace.shape
    return pl.pallas_call(
        power_kernel,
        out_shape=jax.ShapeDtypeStruct(subspace.shape, jnp.float32),
        grid=(freq_count,),
        in_specs=[
            pl.BlockSpec((1, width, width), lambda i: (i, 0, 0)),
            pl.BlockSpec((1, basis, width), lambda i: (i, 0, 0)),
        ],
        out_specs=pl.BlockSpec((1, basis, width), lambda i: (i, 0, 0)),
    )(cov_block, subspace)


def counts_along(places, lags, limit):
    total = jnp.zeros(places.shape, jnp.float32)
    for shift_by in range(lags):
        inside = (places - shift_by >= 0) & (places - shift_by < limit)
        total = total + inside.astype(jnp.float32)
    return total


def on_device(traces, kept_bins, start_basis):
    space_count = lax.axis_size("space")
    cosines, sines = tables(kept_bins)
    dft_scale = 1.0 / math.sqrt(NT)
    waves = jnp.stack([cosines * dft_scale, -sines * dft_scale], axis=1)
    spectra_tile = product("xyt,tcf->fcxy", traces, waves)
    slices = lax.all_to_all(spectra_tile, "freq", split_axis=0, concat_axis=3, tiled=True)
    freq_count = slices.shape[0]
    strip_width = slices.shape[2]
    trace_cols = slices.shape[3]
    rows = LX * LY
    x_offset = lax.axis_index("space") * strip_width
    places = x_offset + jnp.arange(strip_width, dtype=jnp.int32)
    columns = jnp.arange(trace_cols, dtype=jnp.int32)
    limit_x = strip_width * space_count - LX + 1
    limit_y = trace_cols - LY + 1
    valid_x = (places < limit_x).astype(jnp.float32)
    counts = (
        counts_along(places, LX, limit_x)[:, None] * counts_along(columns, LY, limit_y)[None, :]
    )
    lag_shift = shift_matrix(trace_cols, LY, limit_y)
    subspace = paired(start_basis)
    for cadzow_step in range(CADZOW):
        rim_rows = shifted(slices[:, :, : LX - 1, :], "space", -1)
        extended = jnp.concatenate([slices, rim_rows], axis=2)
        lagged = product("fcpz,zby->fcbpy", extended, lag_shift)
        matrix = jnp.stack(
            [lagged[:, :, :, lag_x : lag_x + strip_width, :] for lag_x in range(LX)], axis=2
        )
        matrix = matrix * valid_x[:, None]
        matrix = matrix.reshape(freq_count, 2 * rows, strip_width * trace_cols)
        gram_h = product("fik,fjk->fij", matrix, matrix)
        cov_real = gram_h[:, :rows, :rows] + gram_h[:, rows:, rows:]
        cov_imag = gram_h[:, rows:, :rows] - gram_h[:, :rows, rows:]
        cov = all_sum(jnp.stack([cov_real, cov_imag], axis=1), "space")
        cov_block = realified(cov[:, 0], cov[:, 1])
        subspace = power_steps(cov_block, subspace)
        gram_q = product("fjk,fjl->fkl", subspace, subspace)
        proj_real = 0.5 * (gram_q[:, :rows, :rows] + gram_q[:, rows:, rows:])
        proj_imag = 0.5 * (gram_q[:, rows:, :rows] - gram_q[:, :rows, rows:])
        projected = product("fij,fjk->fik", realified(proj_real, proj_imag), matrix)
        projected = projected.reshape(freq_count, 2, LX, LY, strip_width, trace_cols)
        along_y = product("fcabxy,vby->fcaxv", projected, lag_shift)
        full = sum(
            jnp.pad(along_y[:, :, lag_x], ((0, 0), (0, 0), (lag_x, LX - 1 - lag_x), (0, 0)))
            for lag_x in range(LX)
        )
        spill = shifted(full[:, :, strip_width:, :], "space", 1)
        spill = jnp.pad(spill, ((0, 0), (0, 0), (0, strip_width - (LX - 1)), (0, 0)))
        slices = (full[:, :, :strip_width, :] + spill) / counts
    out_scale = math.sqrt(2.0 / kept_bins.shape[0])
    received = lax.all_to_all(slices, "freq", split_axis=3, concat_axis=0, tiled=True)
    synth = product("fxy,tf->xyt", received[:, 0], cosines)
    synth = synth - product("fxy,tf->xyt", received[:, 1], sines)
    return out_scale * synth


def solution(mesh):
    placed = (P("space", "freq", None), P(), P("freq", None, None, None))
    return jax.shard_map(
        on_device, mesh=mesh, in_specs=placed, out_specs=P("space", "freq", None), check_vma=False
    )
```

```python
import math

import jax
import jax.numpy as jnp
from jax import lax
from jax.experimental import pallas as pl
from jax.sharding import PartitionSpec as P

NT = 2048
LX = 8
LY = 32
RANK = 40
POWER = 4
CADZOW = 2


exact_mode = lax.Precision.HIGHEST


def shifted(x, axis, by):
    count = lax.axis_size(axis)
    pairs = [(i, i + by) for i in range(count) if 0 <= i + by < count]
    return lax.ppermute(x, axis, pairs)


def all_sum(x, axis):
    count = lax.axis_size(axis)
    chunks = x.reshape(count, -1)
    mine = lax.all_to_all(chunks, axis, 0, 0, tiled=True).sum(axis=0)
    copies = jnp.broadcast_to(mine[None], (count, mine.shape[0]))
    return lax.all_to_all(copies, axis, 0, 0, tiled=True).reshape(x.shape)


def product(form, left, right):
    return jnp.einsum(form, left, right, precision=exact_mode, preferred_element_type=jnp.float32)


def tables(kept_bins):
    samples = jnp.arange(NT, dtype=jnp.int32)
    phases = samples[:, None] * kept_bins[None, :] % NT
    angles = phases.astype(jnp.float32) * (2.0 * math.pi / NT)
    return (jnp.cos(angles), jnp.sin(angles))


def paired(start):
    real_rows = jnp.concatenate([start[:, 0], -start[:, 1]], axis=1)
    imag_rows = jnp.concatenate([start[:, 1], start[:, 0]], axis=1)
    return jnp.concatenate([real_rows, imag_rows], axis=2)


def shift_matrix(length, lags, limit):
    shape = (length, lags, length)
    z = lax.broadcasted_iota(jnp.int32, shape, 0)
    b = lax.broadcasted_iota(jnp.int32, shape, 1)
    y = lax.broadcasted_iota(jnp.int32, shape, 2)
    return ((z == y + b) & (y < limit)).astype(jnp.float32)


def realified(real_part, imag_part):
    top = jnp.concatenate([real_part, -imag_part], axis=-1)
    bottom = jnp.concatenate([imag_part, real_part], axis=-1)
    return jnp.concatenate([top, bottom], axis=-2)


def inverse_factor(left_real, left_imag):
    count = left_real.shape[0]
    row_id = lax.broadcasted_iota(jnp.int32, left_real.shape, 0)
    col_id = lax.broadcasted_iota(jnp.int32, left_real.shape, 1)
    eye = (row_id == col_id).astype(jnp.float32)
    rows_only = row_id[:, :1]

    def body(k, carry):
        ar, ai, xr, xi, pivots = carry
        at_row = row_id == k
        at_col = col_id == k
        cr = jnp.sum(jnp.where(at_col, ar, 0.0), axis=1, keepdims=True)
        ci = jnp.sum(jnp.where(at_col, ai, 0.0), axis=1, keepdims=True)
        rr = jnp.sum(jnp.where(at_row, ar, 0.0), axis=0, keepdims=True)
        ri = jnp.sum(jnp.where(at_row, ai, 0.0), axis=0, keepdims=True)
        xrr = jnp.sum(jnp.where(at_row, xr, 0.0), axis=0, keepdims=True)
        xri = jnp.sum(jnp.where(at_row, xi, 0.0), axis=0, keepdims=True)
        pivot = jnp.sum(jnp.where(rows_only == k, cr, 0.0), axis=0, keepdims=True)
        scale = 1.0 / pivot
        below = rows_only > k
        br = jnp.where(below, cr, 0.0) * scale
        bi = jnp.where(below, ci, 0.0) * scale
        ar = ar - (br * rr - bi * ri)
        ai = ai - (br * ri + bi * rr)
        xr = xr - (br * xrr - bi * xri)
        xi = xi - (br * xri + bi * xrr)
        pivots = jnp.where(rows_only == k, pivot, pivots)
        return ar, ai, xr, xi, pivots

    start = (left_real, left_imag, eye, jnp.zeros_like(eye), jnp.zeros((count, 1), jnp.float32))
    _, _, xr, xi, pivots = lax.fori_loop(0, count, body, start)
    norm = lax.rsqrt(pivots)
    return xr * norm, xi * norm


def turned(rows):
    width = rows.shape[1] // 2
    return jnp.concatenate([-rows[:, width:], rows[:, :width]], axis=1)


def power_kernel(cov_ref, start_ref, out_ref):
    cov = cov_ref[0]
    half = start_ref.shape[1] // 2
    subspace = start_ref[0, :half, :]
    contract = (((1,), (1,)), ((), ()))
    for power_step in range(POWER):
        summed = jnp.dot(subspace, cov, precision=exact_mode, preferred_element_type=jnp.float32)
        times_i = turned(summed)
        gram_real = lax.dot_general(
            summed, summed, contract, precision=exact_mode, preferred_element_type=jnp.float32
        )
        gram_imag = -lax.dot_general(
            times_i, summed, contract, precision=exact_mode, preferred_element_type=jnp.float32
        )
        inverse_real, inverse_imag = inverse_factor(gram_real, gram_imag)
        subspace = jnp.dot(
            inverse_real, summed, precision=exact_mode, preferred_element_type=jnp.float32
        ) + jnp.dot(inverse_imag, times_i, precision=exact_mode, preferred_element_type=jnp.float32)
    out_ref[0, :half, :] = subspace
    out_ref[0, half:, :] = turned(subspace)


def power_steps(cov_block, subspace):
    freq_count, basis, width = subspace.shape
    return pl.pallas_call(
        power_kernel,
        out_shape=jax.ShapeDtypeStruct(subspace.shape, jnp.float32),
        grid=(freq_count,),
        in_specs=[
            pl.BlockSpec((1, width, width), lambda i: (i, 0, 0)),
            pl.BlockSpec((1, basis, width), lambda i: (i, 0, 0)),
        ],
        out_specs=pl.BlockSpec((1, basis, width), lambda i: (i, 0, 0)),
    )(cov_block, subspace)


def counts_along(places, lags, limit):
    total = jnp.zeros(places.shape, jnp.float32)
    for shift_by in range(lags):
        inside = (places - shift_by >= 0) & (places - shift_by < limit)
        total = total + inside.astype(jnp.float32)
    return total


def on_device(traces, kept_bins, start_basis):
    space_count = lax.axis_size("space")
    cosines, sines = tables(kept_bins)
    dft_scale = 1.0 / math.sqrt(NT)
    waves = jnp.stack([cosines * dft_scale, -sines * dft_scale], axis=1)
    spectra_tile = product("xyt,tcf->fcxy", traces, waves)
    slices = lax.all_to_all(spectra_tile, "freq", split_axis=0, concat_axis=3, tiled=True)
    freq_count = slices.shape[0]
    strip_width = slices.shape[2]
    trace_cols = slices.shape[3]
    rows = LX * LY
    x_offset = lax.axis_index("space") * strip_width
    places = x_offset + jnp.arange(strip_width, dtype=jnp.int32)
    columns = jnp.arange(trace_cols, dtype=jnp.int32)
    limit_x = strip_width * space_count - LX + 1
    limit_y = trace_cols - LY + 1
    valid_x = (places < limit_x).astype(jnp.float32)
    counts = (
        counts_along(places, LX, limit_x)[:, None] * counts_along(columns, LY, limit_y)[None, :]
    )
    lag_shift = shift_matrix(trace_cols, LY, limit_y)
    subspace = paired(start_basis)
    for cadzow_step in range(CADZOW):
        rim_rows = shifted(slices[:, :, : LX - 1, :], "space", -1)
        extended = jnp.concatenate([slices, rim_rows], axis=2)
        lagged = product("fcpz,zby->fcbpy", extended, lag_shift)
        matrix = jnp.stack(
            [lagged[:, :, :, lag_x : lag_x + strip_width, :] for lag_x in range(LX)], axis=2
        )
        matrix = matrix * valid_x[:, None]
        matrix = matrix.reshape(freq_count, 2 * rows, strip_width * trace_cols)
        gram_h = product("fik,fjk->fij", matrix, matrix)
        cov_real = gram_h[:, :rows, :rows] + gram_h[:, rows:, rows:]
        cov_imag = gram_h[:, rows:, :rows] - gram_h[:, :rows, rows:]
        cov = all_sum(jnp.stack([cov_real, cov_imag], axis=1), "space")
        cov_block = realified(cov[:, 0], cov[:, 1])
        subspace = power_steps(cov_block, subspace)
        gram_q = product("fjk,fjl->fkl", subspace, subspace)
        proj_real = 0.5 * (gram_q[:, :rows, :rows] + gram_q[:, rows:, rows:])
        proj_imag = 0.5 * (gram_q[:, rows:, :rows] - gram_q[:, :rows, rows:])
        projected = product("fij,fjk->fik", realified(proj_real, proj_imag), matrix)
        projected = projected.reshape(freq_count, 2, LX, LY, strip_width, trace_cols)
        along_y = product("fcabxy,vby->fcaxv", projected, lag_shift)
        full = sum(
            jnp.pad(along_y[:, :, lag_x], ((0, 0), (0, 0), (lag_x, LX - 1 - lag_x), (0, 0)))
            for lag_x in range(LX)
        )
        spill = shifted(full[:, :, strip_width:, :], "space", 1)
        spill = jnp.pad(spill, ((0, 0), (0, 0), (0, strip_width - (LX - 1)), (0, 0)))
        slices = (full[:, :, :strip_width, :] + spill) / counts
    out_scale = math.sqrt(2.0 / kept_bins.shape[0])
    received = lax.all_to_all(slices, "freq", split_axis=3, concat_axis=0, tiled=True)
    synth = product("fxy,tf->xyt", received[:, 0], cosines)
    synth = synth - product("fxy,tf->xyt", received[:, 1], sines)
    return out_scale * synth


def solution(mesh):
    placed = (P("space", "freq", None), P(), P("freq", None, None, None))
    return jax.shard_map(
        on_device, mesh=mesh, in_specs=placed, out_specs=P("space", "freq", None), check_vma=False
    )
```

```python
import math

import jax
import jax.numpy as jnp
from jax import lax
from jax.experimental import pallas as pl
from jax.sharding import PartitionSpec as P

NT = 2048
LX = 8
LY = 32
RANK = 40
POWER = 4
CADZOW = 2


exact_mode = lax.Precision.HIGHEST


def shifted(x, axis, by):
    count = lax.axis_size(axis)
    pairs = [(i, i + by) for i in range(count) if 0 <= i + by < count]
    return lax.ppermute(x, axis, pairs)


def all_sum(x, axis):
    count = lax.axis_size(axis)
    chunks = x.reshape(count, -1)
    mine = lax.all_to_all(chunks, axis, 0, 0, tiled=True).sum(axis=0)
    copies = jnp.broadcast_to(mine[None], (count, mine.shape[0]))
    return lax.all_to_all(copies, axis, 0, 0, tiled=True).reshape(x.shape)


def product(form, left, right):
    return jnp.einsum(form, left, right, precision=exact_mode, preferred_element_type=jnp.float32)


def tables(kept_bins):
    samples = jnp.arange(NT, dtype=jnp.int32)
    phases = samples[:, None] * kept_bins[None, :] % NT
    angles = phases.astype(jnp.float32) * (2.0 * math.pi / NT)
    return (jnp.cos(angles), jnp.sin(angles))


def paired(start):
    real_rows = jnp.concatenate([start[:, 0], -start[:, 1]], axis=1)
    imag_rows = jnp.concatenate([start[:, 1], start[:, 0]], axis=1)
    return jnp.concatenate([real_rows, imag_rows], axis=2)


def shift_matrix(length, lags, limit):
    shape = (length, lags, length)
    z = lax.broadcasted_iota(jnp.int32, shape, 0)
    b = lax.broadcasted_iota(jnp.int32, shape, 1)
    y = lax.broadcasted_iota(jnp.int32, shape, 2)
    return ((z == y + b) & (y < limit)).astype(jnp.float32)


def realified(real_part, imag_part):
    top = jnp.concatenate([real_part, -imag_part], axis=-1)
    bottom = jnp.concatenate([imag_part, real_part], axis=-1)
    return jnp.concatenate([top, bottom], axis=-2)


def packed(real_part, imag_part):
    upper = lax.broadcasted_iota(jnp.int32, real_part.shape, real_part.ndim - 2) <= lax.broadcasted_iota(
        jnp.int32, real_part.shape, real_part.ndim - 1
    )
    return jnp.where(upper, real_part, imag_part)


def unpacked(square):
    row_id = lax.broadcasted_iota(jnp.int32, square.shape, square.ndim - 2)
    col_id = lax.broadcasted_iota(jnp.int32, square.shape, square.ndim - 1)
    mirrored = jnp.swapaxes(square, -1, -2)
    real_part = jnp.where(row_id <= col_id, square, mirrored)
    imag_part = jnp.where(row_id > col_id, square, jnp.where(row_id == col_id, 0.0, -mirrored))
    return real_part, imag_part


def inverse_factor(left_real, left_imag):
    count = left_real.shape[0]
    row_id = lax.broadcasted_iota(jnp.int32, left_real.shape, 0)
    col_id = lax.broadcasted_iota(jnp.int32, left_real.shape, 1)
    eye = (row_id == col_id).astype(jnp.float32)
    rows_only = row_id[:, :1]

    def body(k, carry):
        ar, ai, xr, xi, pivots = carry
        at_row = row_id == k
        at_col = col_id == k
        cr = jnp.sum(jnp.where(at_col, ar, 0.0), axis=1, keepdims=True)
        ci = jnp.sum(jnp.where(at_col, ai, 0.0), axis=1, keepdims=True)
        rr = jnp.sum(jnp.where(at_row, ar, 0.0), axis=0, keepdims=True)
        ri = jnp.sum(jnp.where(at_row, ai, 0.0), axis=0, keepdims=True)
        xrr = jnp.sum(jnp.where(at_row, xr, 0.0), axis=0, keepdims=True)
        xri = jnp.sum(jnp.where(at_row, xi, 0.0), axis=0, keepdims=True)
        pivot = jnp.sum(jnp.where(rows_only == k, cr, 0.0), axis=0, keepdims=True)
        scale = 1.0 / pivot
        below = rows_only > k
        br = jnp.where(below, cr, 0.0) * scale
        bi = jnp.where(below, ci, 0.0) * scale
        ar = ar - (br * rr - bi * ri)
        ai = ai - (br * ri + bi * rr)
        xr = xr - (br * xrr - bi * xri)
        xi = xi - (br * xri + bi * xrr)
        pivots = jnp.where(rows_only == k, pivot, pivots)
        return ar, ai, xr, xi, pivots

    start = (left_real, left_imag, eye, jnp.zeros_like(eye), jnp.zeros((count, 1), jnp.float32))
    _, _, xr, xi, pivots = lax.fori_loop(0, count, body, start)
    norm = lax.rsqrt(pivots)
    return xr * norm, xi * norm


def turned(rows):
    width = rows.shape[1] // 2
    return jnp.concatenate([-rows[:, width:], rows[:, :width]], axis=1)


def power_kernel(cov_ref, start_ref, out_ref):
    cov = cov_ref[0]
    half = start_ref.shape[1] // 2
    subspace = start_ref[0, :half, :]
    contract = (((1,), (1,)), ((), ()))
    for power_step in range(POWER):
        summed = jnp.dot(subspace, cov, precision=exact_mode, preferred_element_type=jnp.float32)
        times_i = turned(summed)
        gram_real = lax.dot_general(
            summed, summed, contract, precision=exact_mode, preferred_element_type=jnp.float32
        )
        gram_imag = -lax.dot_general(
            times_i, summed, contract, precision=exact_mode, preferred_element_type=jnp.float32
        )
        inverse_real, inverse_imag = inverse_factor(gram_real, gram_imag)
        subspace = jnp.dot(
            inverse_real, summed, precision=exact_mode, preferred_element_type=jnp.float32
        ) + jnp.dot(inverse_imag, times_i, precision=exact_mode, preferred_element_type=jnp.float32)
    out_ref[0, :half, :] = subspace
    out_ref[0, half:, :] = turned(subspace)


def power_steps(cov_block, subspace):
    freq_count, basis, width = subspace.shape
    return pl.pallas_call(
        power_kernel,
        out_shape=jax.ShapeDtypeStruct(subspace.shape, jnp.float32),
        grid=(freq_count,),
        in_specs=[
            pl.BlockSpec((1, width, width), lambda i: (i, 0, 0)),
            pl.BlockSpec((1, basis, width), lambda i: (i, 0, 0)),
        ],
        out_specs=pl.BlockSpec((1, basis, width), lambda i: (i, 0, 0)),
    )(cov_block, subspace)


def counts_along(places, lags, limit):
    total = jnp.zeros(places.shape, jnp.float32)
    for shift_by in range(lags):
        inside = (places - shift_by >= 0) & (places - shift_by < limit)
        total = total + inside.astype(jnp.float32)
    return total


def on_device(traces, kept_bins, start_basis):
    space_count = lax.axis_size("space")
    cosines, sines = tables(kept_bins)
    dft_scale = 1.0 / math.sqrt(NT)
    waves = jnp.stack([cosines * dft_scale, -sines * dft_scale], axis=1)
    spectra_tile = product("xyt,tcf->fcxy", traces, waves)
    slices = lax.all_to_all(spectra_tile, "freq", split_axis=0, concat_axis=3, tiled=True)
    freq_count = slices.shape[0]
    strip_width = slices.shape[2]
    trace_cols = slices.shape[3]
    rows = LX * LY
    x_offset = lax.axis_index("space") * strip_width
    places = x_offset + jnp.arange(strip_width, dtype=jnp.int32)
    columns = jnp.arange(trace_cols, dtype=jnp.int32)
    limit_x = strip_width * space_count - LX + 1
    limit_y = trace_cols - LY + 1
    valid_x = (places < limit_x).astype(jnp.float32)
    counts = (
        counts_along(places, LX, limit_x)[:, None] * counts_along(columns, LY, limit_y)[None, :]
    )
    lag_shift = shift_matrix(trace_cols, LY, limit_y)
    subspace = paired(start_basis)
    next_counts = (
        counts_along(places + strip_width, LX, limit_x)[:, None]
        * counts_along(columns, LY, limit_y)[None, :]
    )[: LX - 1]
    next_counts = jnp.maximum(next_counts, 1.0)
    rim_rows = shifted(slices[:, :, : LX - 1, :], "space", -1)
    for cadzow_step in range(CADZOW):
        extended = jnp.concatenate([slices, rim_rows], axis=2)
        lagged = product("fcpz,zby->fcbpy", extended, lag_shift)
        matrix = jnp.stack(
            [lagged[:, :, :, lag_x : lag_x + strip_width, :] for lag_x in range(LX)], axis=2
        )
        matrix = matrix * valid_x[:, None]
        matrix = matrix.reshape(freq_count, 2 * rows, strip_width * trace_cols)
        gram_h = product("fik,fjk->fij", matrix, matrix)
        cov_real = gram_h[:, :rows, :rows] + gram_h[:, rows:, rows:]
        cov_imag = gram_h[:, rows:, :rows] - gram_h[:, :rows, rows:]
        cov = all_sum(packed(cov_real, cov_imag), "space")
        cov_block = realified(*unpacked(cov))
        subspace = power_steps(cov_block, subspace)
        gram_q = product("fjk,fjl->fkl", subspace, subspace)
        proj_real = 0.5 * (gram_q[:, :rows, :rows] + gram_q[:, rows:, rows:])
        proj_imag = 0.5 * (gram_q[:, rows:, :rows] - gram_q[:, :rows, rows:])
        projected = product("fij,fjk->fik", realified(proj_real, proj_imag), matrix)
        projected = projected.reshape(freq_count, 2, LX, LY, strip_width, trace_cols)
        along_y = product("fcabxy,vby->fcaxv", projected, lag_shift)
        full = sum(
            jnp.pad(along_y[:, :, lag_x], ((0, 0), (0, 0), (lag_x, LX - 1 - lag_x), (0, 0)))
            for lag_x in range(LX)
        )
        tail = full[:, :, strip_width:, :]
        spill = shifted(tail, "space", 1)
        if cadzow_step + 1 < CADZOW:
            next_head = shifted(full[:, :, : LX - 1, :], "space", -1)
            rim_rows = (next_head + tail) / next_counts
        spill = jnp.pad(spill, ((0, 0), (0, 0), (0, strip_width - (LX - 1)), (0, 0)))
        slices = (full[:, :, :strip_width, :] + spill) / counts
    out_scale = math.sqrt(2.0 / kept_bins.shape[0])
    received = lax.all_to_all(slices, "freq", split_axis=3, concat_axis=0, tiled=True)
    synth = product("fxy,tf->xyt", received[:, 0], cosines)
    synth = synth - product("fxy,tf->xyt", received[:, 1], sines)
    return out_scale * synth


def solution(mesh):
    placed = (P("space", "freq", None), P(), P("freq", None, None, None))
    return jax.shard_map(
        on_device, mesh=mesh, in_specs=placed, out_specs=P("space", "freq", None), check_vma=False
    )
```

```python
import math

import jax
import jax.numpy as jnp
from jax import lax
from jax.experimental import pallas as pl
from jax.sharding import PartitionSpec as P

NT = 2048
LX = 8
LY = 32
RANK = 40
POWER = 4
CADZOW = 2


exact_mode = lax.Precision.HIGHEST


def shifted(x, axis, by):
    count = lax.axis_size(axis)
    pairs = [(i, i + by) for i in range(count) if 0 <= i + by < count]
    return lax.ppermute(x, axis, pairs)


def all_sum(x, axis):
    count = lax.axis_size(axis)
    chunks = x.reshape(count, -1)
    mine = lax.all_to_all(chunks, axis, 0, 0, tiled=True).sum(axis=0)
    copies = jnp.broadcast_to(mine[None], (count, mine.shape[0]))
    return lax.all_to_all(copies, axis, 0, 0, tiled=True).reshape(x.shape)


def product(form, left, right):
    return jnp.einsum(form, left, right, precision=exact_mode, preferred_element_type=jnp.float32)


def tables(kept_bins):
    samples = jnp.arange(NT, dtype=jnp.int32)
    phases = samples[:, None] * kept_bins[None, :] % NT
    angles = phases.astype(jnp.float32) * (2.0 * math.pi / NT)
    return (jnp.cos(angles), jnp.sin(angles))


def paired(start):
    real_rows = jnp.concatenate([start[:, 0], -start[:, 1]], axis=1)
    imag_rows = jnp.concatenate([start[:, 1], start[:, 0]], axis=1)
    return jnp.concatenate([real_rows, imag_rows], axis=2)


def shift_matrix(length, lags, limit):
    shape = (length, lags, length)
    z = lax.broadcasted_iota(jnp.int32, shape, 0)
    b = lax.broadcasted_iota(jnp.int32, shape, 1)
    y = lax.broadcasted_iota(jnp.int32, shape, 2)
    return ((z == y + b) & (y < limit)).astype(jnp.float32)


def realified(real_part, imag_part):
    top = jnp.concatenate([real_part, -imag_part], axis=-1)
    bottom = jnp.concatenate([imag_part, real_part], axis=-1)
    return jnp.concatenate([top, bottom], axis=-2)


def packed(real_part, imag_part):
    upper = lax.broadcasted_iota(jnp.int32, real_part.shape, real_part.ndim - 2) <= lax.broadcasted_iota(
        jnp.int32, real_part.shape, real_part.ndim - 1
    )
    return jnp.where(upper, real_part, imag_part)


def unpacked(square):
    row_id = lax.broadcasted_iota(jnp.int32, square.shape, square.ndim - 2)
    col_id = lax.broadcasted_iota(jnp.int32, square.shape, square.ndim - 1)
    mirrored = jnp.swapaxes(square, -1, -2)
    real_part = jnp.where(row_id <= col_id, square, mirrored)
    imag_part = jnp.where(row_id > col_id, square, jnp.where(row_id == col_id, 0.0, -mirrored))
    return real_part, imag_part


def inverse_factor(left_real, left_imag):
    count = left_real.shape[0]
    row_id = lax.broadcasted_iota(jnp.int32, left_real.shape, 0)
    col_id = lax.broadcasted_iota(jnp.int32, left_real.shape, 1)
    eye = (row_id == col_id).astype(jnp.float32)
    rows_only = row_id[:, :1]

    def body(k, carry):
        ar, ai, xr, xi, pivots = carry
        at_row = row_id == k
        at_col = col_id == k
        cr = jnp.sum(jnp.where(at_col, ar, 0.0), axis=1, keepdims=True)
        ci = jnp.sum(jnp.where(at_col, ai, 0.0), axis=1, keepdims=True)
        rr = jnp.sum(jnp.where(at_row, ar, 0.0), axis=0, keepdims=True)
        ri = jnp.sum(jnp.where(at_row, ai, 0.0), axis=0, keepdims=True)
        xrr = jnp.sum(jnp.where(at_row, xr, 0.0), axis=0, keepdims=True)
        xri = jnp.sum(jnp.where(at_row, xi, 0.0), axis=0, keepdims=True)
        pivot = jnp.sum(jnp.where(rows_only == k, cr, 0.0), axis=0, keepdims=True)
        scale = 1.0 / pivot
        below = rows_only > k
        br = jnp.where(below, cr, 0.0) * scale
        bi = jnp.where(below, ci, 0.0) * scale
        ar = ar - (br * rr - bi * ri)
        ai = ai - (br * ri + bi * rr)
        xr = xr - (br * xrr - bi * xri)
        xi = xi - (br * xri + bi * xrr)
        pivots = jnp.where(rows_only == k, pivot, pivots)
        return ar, ai, xr, xi, pivots

    start = (left_real, left_imag, eye, jnp.zeros_like(eye), jnp.zeros((count, 1), jnp.float32))
    _, _, xr, xi, pivots = lax.fori_loop(0, count, body, start)
    norm = lax.rsqrt(pivots)
    return xr * norm, xi * norm


def turned(rows):
    width = rows.shape[1] // 2
    return jnp.concatenate([-rows[:, width:], rows[:, :width]], axis=1)


def power_kernel(cov_ref, start_ref, out_ref):
    cov = cov_ref[0]
    half = start_ref.shape[1] // 2
    subspace = start_ref[0, :half, :]
    contract = (((1,), (1,)), ((), ()))
    for power_step in range(POWER):
        summed = jnp.dot(subspace, cov, precision=exact_mode, preferred_element_type=jnp.float32)
        times_i = turned(summed)
        gram_real = lax.dot_general(
            summed, summed, contract, precision=exact_mode, preferred_element_type=jnp.float32
        )
        gram_imag = -lax.dot_general(
            times_i, summed, contract, precision=exact_mode, preferred_element_type=jnp.float32
        )
        inverse_real, inverse_imag = inverse_factor(gram_real, gram_imag)
        subspace = jnp.dot(
            inverse_real, summed, precision=exact_mode, preferred_element_type=jnp.float32
        ) + jnp.dot(inverse_imag, times_i, precision=exact_mode, preferred_element_type=jnp.float32)
    out_ref[0, :half, :] = subspace
    out_ref[0, half:, :] = turned(subspace)


def power_steps(cov_block, subspace):
    freq_count, basis, width = subspace.shape
    return pl.pallas_call(
        power_kernel,
        out_shape=jax.ShapeDtypeStruct(subspace.shape, jnp.float32),
        grid=(freq_count,),
        in_specs=[
            pl.BlockSpec((1, width, width), lambda i: (i, 0, 0)),
            pl.BlockSpec((1, basis, width), lambda i: (i, 0, 0)),
        ],
        out_specs=pl.BlockSpec((1, basis, width), lambda i: (i, 0, 0)),
    )(cov_block, subspace)


def counts_along(places, lags, limit):
    total = jnp.zeros(places.shape, jnp.float32)
    for shift_by in range(lags):
        inside = (places - shift_by >= 0) & (places - shift_by < limit)
        total = total + inside.astype(jnp.float32)
    return total


def on_device(traces, kept_bins, start_basis):
    space_count = lax.axis_size("space")
    cosines, sines = tables(kept_bins)
    dft_scale = 1.0 / math.sqrt(NT)
    waves = jnp.stack([cosines * dft_scale, -sines * dft_scale], axis=1)
    spectra_tile = product("xyt,tcf->fcxy", traces, waves)
    slices = lax.all_to_all(spectra_tile, "freq", split_axis=0, concat_axis=3, tiled=True)
    freq_count = slices.shape[0]
    strip_width = slices.shape[2]
    trace_cols = slices.shape[3]
    rows = LX * LY
    x_offset = lax.axis_index("space") * strip_width
    places = x_offset + jnp.arange(strip_width, dtype=jnp.int32)
    columns = jnp.arange(trace_cols, dtype=jnp.int32)
    limit_x = strip_width * space_count - LX + 1
    limit_y = trace_cols - LY + 1
    valid_x = (places < limit_x).astype(jnp.float32)
    counts = (
        counts_along(places, LX, limit_x)[:, None] * counts_along(columns, LY, limit_y)[None, :]
    )
    lag_shift = shift_matrix(trace_cols, LY, limit_y)
    subspace = paired(start_basis)
    next_counts = (
        counts_along(places + strip_width, LX, limit_x)[:, None]
        * counts_along(columns, LY, limit_y)[None, :]
    )[: LX - 1]
    next_counts = jnp.maximum(next_counts, 1.0)
    rim_rows = shifted(slices[:, :, : LX - 1, :], "space", -1)
    for cadzow_step in range(CADZOW):
        extended = jnp.concatenate([slices, rim_rows], axis=2)
        lagged = product("fcpz,zby->fcbpy", extended, lag_shift)
        matrix = jnp.stack(
            [lagged[:, :, :, lag_x : lag_x + strip_width, :] for lag_x in range(LX)], axis=2
        )
        matrix = matrix * valid_x[:, None]
        matrix = matrix.reshape(freq_count, 2 * rows, strip_width * trace_cols)
        gram_h = product("fik,fjk->fij", matrix, matrix)
        cov_real = gram_h[:, :rows, :rows] + gram_h[:, rows:, rows:]
        cov_imag = gram_h[:, rows:, :rows] - gram_h[:, :rows, rows:]
        cov = all_sum(packed(cov_real, cov_imag), "space")
        cov_block = realified(*unpacked(cov))
        subspace = power_steps(cov_block, subspace)
        half = subspace.shape[1] // 2
        signs = jnp.where(jnp.arange(2 * half) < half, 1.0, -1.0)[:, None]
        weights = subspace * signs
        coeffs = product("fjk,fkc->fjc", weights, matrix)
        projected = product("fjk,fjc->fkc", weights, coeffs)
        projected = projected.reshape(freq_count, 2, LX, LY, strip_width, trace_cols)
        along_y = product("fcabxy,vby->fcaxv", projected, lag_shift)
        full = sum(
            jnp.pad(along_y[:, :, lag_x], ((0, 0), (0, 0), (lag_x, LX - 1 - lag_x), (0, 0)))
            for lag_x in range(LX)
        )
        tail = full[:, :, strip_width:, :]
        spill = shifted(tail, "space", 1)
        if cadzow_step + 1 < CADZOW:
            next_head = shifted(full[:, :, : LX - 1, :], "space", -1)
            rim_rows = (next_head + tail) / next_counts
        spill = jnp.pad(spill, ((0, 0), (0, 0), (0, strip_width - (LX - 1)), (0, 0)))
        slices = (full[:, :, :strip_width, :] + spill) / counts
    out_scale = math.sqrt(2.0 / kept_bins.shape[0])
    received = lax.all_to_all(slices, "freq", split_axis=3, concat_axis=0, tiled=True)
    synth = product("fxy,tf->xyt", received[:, 0], cosines)
    synth = synth - product("fxy,tf->xyt", received[:, 1], sines)
    return out_scale * synth


def solution(mesh):
    placed = (P("space", "freq", None), P(), P("freq", None, None, None))
    return jax.shard_map(
        on_device, mesh=mesh, in_specs=placed, out_specs=P("space", "freq", None), check_vma=False
    )
```

```python
import math

import jax
import jax.numpy as jnp
from jax import lax
from jax.experimental import pallas as pl
from jax.experimental.pallas import tpu as pltpu
from jax.sharding import PartitionSpec as P

NT = 2048
LX = 8
LY = 32
RANK = 40
POWER = 4
CADZOW = 2


exact_mode = lax.Precision.HIGHEST


def shifted(x, axis, by):
    count = lax.axis_size(axis)
    pairs = [(i, i + by) for i in range(count) if 0 <= i + by < count]
    return lax.ppermute(x, axis, pairs)


def all_sum(x, axis):
    count = lax.axis_size(axis)
    chunks = x.reshape(count, -1)
    mine = lax.all_to_all(chunks, axis, 0, 0, tiled=True).sum(axis=0)
    copies = jnp.broadcast_to(mine[None], (count, mine.shape[0]))
    return lax.all_to_all(copies, axis, 0, 0, tiled=True).reshape(x.shape)


def product(form, left, right):
    return jnp.einsum(form, left, right, precision=exact_mode, preferred_element_type=jnp.float32)


def tables(kept_bins):
    samples = jnp.arange(NT, dtype=jnp.int32)
    phases = samples[:, None] * kept_bins[None, :] % NT
    angles = phases.astype(jnp.float32) * (2.0 * math.pi / NT)
    return (jnp.cos(angles), jnp.sin(angles))


def paired(start):
    real_rows = jnp.concatenate([start[:, 0], -start[:, 1]], axis=1)
    imag_rows = jnp.concatenate([start[:, 1], start[:, 0]], axis=1)
    return jnp.concatenate([real_rows, imag_rows], axis=2)


def shift_matrix(length, lags, limit):
    shape = (length, lags, length)
    z = lax.broadcasted_iota(jnp.int32, shape, 0)
    b = lax.broadcasted_iota(jnp.int32, shape, 1)
    y = lax.broadcasted_iota(jnp.int32, shape, 2)
    return ((z == y + b) & (y < limit)).astype(jnp.float32)


def realified(real_part, imag_part):
    top = jnp.concatenate([real_part, -imag_part], axis=-1)
    bottom = jnp.concatenate([imag_part, real_part], axis=-1)
    return jnp.concatenate([top, bottom], axis=-2)


def packed(real_part, imag_part):
    upper = lax.broadcasted_iota(jnp.int32, real_part.shape, real_part.ndim - 2) <= lax.broadcasted_iota(
        jnp.int32, real_part.shape, real_part.ndim - 1
    )
    return jnp.where(upper, real_part, imag_part)


def unpacked(square):
    row_id = lax.broadcasted_iota(jnp.int32, square.shape, square.ndim - 2)
    col_id = lax.broadcasted_iota(jnp.int32, square.shape, square.ndim - 1)
    mirrored = jnp.swapaxes(square, -1, -2)
    real_part = jnp.where(row_id <= col_id, square, mirrored)
    imag_part = jnp.where(row_id > col_id, square, jnp.where(row_id == col_id, 0.0, -mirrored))
    return real_part, imag_part


def inverse_factor(left):
    count, width = left.shape
    half = width // 2
    row_id = lax.broadcasted_iota(jnp.int32, left.shape, 0)
    lane_id = lax.broadcasted_iota(jnp.int32, left.shape, 1)
    sign = jnp.where(lane_id[:1] < half, -1.0, 1.0)
    rows_only = row_id[:, :1]

    def body(k, carry):
        left, inverse, pivots = carry
        at_row = row_id == k
        col_real = jnp.sum(jnp.where(lane_id == k, left, 0.0), axis=1, keepdims=True)
        col_imag = jnp.sum(jnp.where(lane_id == k + half, left, 0.0), axis=1, keepdims=True)
        row_left = jnp.sum(jnp.where(at_row, left, 0.0), axis=0, keepdims=True)
        row_inverse = jnp.sum(jnp.where(at_row, inverse, 0.0), axis=0, keepdims=True)
        pivot = jnp.sum(jnp.where(rows_only == k, col_real, 0.0), axis=0, keepdims=True)
        scale = 1.0 / pivot
        below = rows_only > k
        by_real = jnp.where(below, col_real, 0.0) * scale
        by_imag = jnp.where(below, col_imag, 0.0) * scale
        left = left - (by_real * row_left + by_imag * (pltpu.roll(row_left, half, 1) * sign))
        inverse = inverse - (
            by_real * row_inverse + by_imag * (pltpu.roll(row_inverse, half, 1) * sign)
        )
        pivots = jnp.where(rows_only == k, pivot, pivots)
        return left, inverse, pivots

    eye = (row_id == lane_id).astype(jnp.float32)
    start = (left, eye, jnp.zeros((count, 1), jnp.float32))
    _, inverse, pivots = lax.fori_loop(0, count, body, start)
    return inverse * lax.rsqrt(pivots)


def turned(rows):
    width = rows.shape[1] // 2
    return jnp.concatenate([-rows[:, width:], rows[:, :width]], axis=1)


def dot(left, right):
    return jnp.dot(left, right, precision=exact_mode, preferred_element_type=jnp.float32)


def power_kernel(cov_ref, start_ref, out_ref):
    square = cov_ref[0]
    mirrored = square.T
    row_id = lax.broadcasted_iota(jnp.int32, square.shape, 0)
    col_id = lax.broadcasted_iota(jnp.int32, square.shape, 1)
    cov_real = jnp.where(row_id <= col_id, square, mirrored)
    cov_imag = jnp.where(row_id > col_id, square, jnp.where(row_id == col_id, 0.0, -mirrored))
    half = start_ref.shape[1] // 2
    width = square.shape[0]
    subspace = start_ref[0, :half, :]
    pad = jnp.zeros((64 - half, 2 * width), jnp.float32)
    contract = (((1,), (1,)), ((), ()))
    for power_step in range(POWER):
        sub_real = subspace[:, :width]
        sub_imag = subspace[:, width:]
        summed = jnp.concatenate(
            [
                dot(sub_real, cov_real) + dot(sub_imag, cov_imag),
                dot(sub_imag, cov_real) - dot(sub_real, cov_imag),
            ],
            axis=1,
        )
        stacked = jnp.concatenate([summed, pad, turned(summed), pad], axis=0)
        gram_matrix = lax.dot_general(
            summed, stacked, contract, precision=exact_mode, preferred_element_type=jnp.float32
        )
        subspace = dot(inverse_factor(gram_matrix), stacked)
    out_ref[0, :half, :] = subspace
    out_ref[0, half:, :] = turned(subspace)


def power_steps(cov_square, subspace):
    freq_count, basis, width = subspace.shape
    rows = cov_square.shape[1]
    return pl.pallas_call(
        power_kernel,
        out_shape=jax.ShapeDtypeStruct(subspace.shape, jnp.float32),
        grid=(freq_count,),
        in_specs=[
            pl.BlockSpec((1, rows, rows), lambda i: (i, 0, 0)),
            pl.BlockSpec((1, basis, width), lambda i: (i, 0, 0)),
        ],
        out_specs=pl.BlockSpec((1, basis, width), lambda i: (i, 0, 0)),
    )(cov_square, subspace)


def counts_along(places, lags, limit):
    total = jnp.zeros(places.shape, jnp.float32)
    for shift_by in range(lags):
        inside = (places - shift_by >= 0) & (places - shift_by < limit)
        total = total + inside.astype(jnp.float32)
    return total


def on_device(traces, kept_bins, start_basis):
    space_count = lax.axis_size("space")
    cosines, sines = tables(kept_bins)
    dft_scale = 1.0 / math.sqrt(NT)
    waves = jnp.stack([cosines * dft_scale, -sines * dft_scale], axis=1)
    spectra_tile = product("xyt,tcf->fcxy", traces, waves)
    slices = lax.all_to_all(spectra_tile, "freq", split_axis=0, concat_axis=3, tiled=True)
    freq_count = slices.shape[0]
    strip_width = slices.shape[2]
    trace_cols = slices.shape[3]
    rows = LX * LY
    x_offset = lax.axis_index("space") * strip_width
    places = x_offset + jnp.arange(strip_width, dtype=jnp.int32)
    columns = jnp.arange(trace_cols, dtype=jnp.int32)
    limit_x = strip_width * space_count - LX + 1
    limit_y = trace_cols - LY + 1
    valid_x = (places < limit_x).astype(jnp.float32)
    counts = (
        counts_along(places, LX, limit_x)[:, None] * counts_along(columns, LY, limit_y)[None, :]
    )
    lag_shift = shift_matrix(trace_cols, LY, limit_y)
    subspace = paired(start_basis)
    next_counts = (
        counts_along(places + strip_width, LX, limit_x)[:, None]
        * counts_along(columns, LY, limit_y)[None, :]
    )[: LX - 1]
    next_counts = jnp.maximum(next_counts, 1.0)
    rim_rows = shifted(slices[:, :, : LX - 1, :], "space", -1)
    for cadzow_step in range(CADZOW):
        extended = jnp.concatenate([slices, rim_rows], axis=2)
        lagged = product("fcpz,zby->fcbpy", extended, lag_shift)
        matrix = jnp.stack(
            [lagged[:, :, :, lag_x : lag_x + strip_width, :] for lag_x in range(LX)], axis=2
        )
        matrix = matrix * valid_x[:, None]
        matrix = matrix.reshape(freq_count, 2 * rows, strip_width * trace_cols)
        gram_h = product("fik,fjk->fij", matrix, matrix)
        cov_real = gram_h[:, :rows, :rows] + gram_h[:, rows:, rows:]
        cov_imag = gram_h[:, rows:, :rows] - gram_h[:, :rows, rows:]
        cov = all_sum(packed(cov_real, cov_imag), "space")
        subspace = power_steps(cov, subspace)
        half = subspace.shape[1] // 2
        signs = jnp.where(jnp.arange(2 * half) < half, 1.0, -1.0)[:, None]
        weights = subspace * signs
        coeffs = product("fjk,fkc->fjc", weights, matrix)
        projected = product("fjk,fjc->fkc", weights, coeffs)
        projected = projected.reshape(freq_count, 2, LX, LY, strip_width, trace_cols)
        along_y = product("fcabxy,vby->fcaxv", projected, lag_shift)
        full = sum(
            jnp.pad(along_y[:, :, lag_x], ((0, 0), (0, 0), (lag_x, LX - 1 - lag_x), (0, 0)))
            for lag_x in range(LX)
        )
        tail = full[:, :, strip_width:, :]
        spill = shifted(tail, "space", 1)
        if cadzow_step + 1 < CADZOW:
            next_head = shifted(full[:, :, : LX - 1, :], "space", -1)
            rim_rows = (next_head + tail) / next_counts
        spill = jnp.pad(spill, ((0, 0), (0, 0), (0, strip_width - (LX - 1)), (0, 0)))
        slices = (full[:, :, :strip_width, :] + spill) / counts
    out_scale = math.sqrt(2.0 / kept_bins.shape[0])
    received = lax.all_to_all(slices, "freq", split_axis=3, concat_axis=0, tiled=True)
    synth = product("fxy,tf->xyt", received[:, 0], cosines)
    synth = synth - product("fxy,tf->xyt", received[:, 1], sines)
    return out_scale * synth


def solution(mesh):
    placed = (P("space", "freq", None), P(), P("freq", None, None, None))
    return jax.shard_map(
        on_device, mesh=mesh, in_specs=placed, out_specs=P("space", "freq", None), check_vma=False
    )
```

```python
import math

import jax
import jax.numpy as jnp
from jax import lax
from jax.experimental import pallas as pl
from jax.experimental.pallas import tpu as pltpu
from jax.sharding import PartitionSpec as P

NT = 2048
LX = 8
LY = 32
RANK = 40
POWER = 4
CADZOW = 2


exact_mode = lax.Precision.HIGHEST


def shifted(x, axis, by):
    count = lax.axis_size(axis)
    pairs = [(i, i + by) for i in range(count) if 0 <= i + by < count]
    return lax.ppermute(x, axis, pairs)


def all_sum(x, axis):
    count = lax.axis_size(axis)
    chunks = x.reshape(count, -1)
    mine = lax.all_to_all(chunks, axis, 0, 0, tiled=True).sum(axis=0)
    copies = jnp.broadcast_to(mine[None], (count, mine.shape[0]))
    return lax.all_to_all(copies, axis, 0, 0, tiled=True).reshape(x.shape)


def product(form, left, right, precision=exact_mode):
    return jnp.einsum(form, left, right, precision=precision, preferred_element_type=jnp.float32)


def tables(kept_bins):
    samples = jnp.arange(NT, dtype=jnp.int32)
    phases = samples[:, None] * kept_bins[None, :] % NT
    angles = phases.astype(jnp.float32) * (2.0 * math.pi / NT)
    return (jnp.cos(angles), jnp.sin(angles))


def paired(start):
    real_rows = jnp.concatenate([start[:, 0], -start[:, 1]], axis=1)
    imag_rows = jnp.concatenate([start[:, 1], start[:, 0]], axis=1)
    return jnp.concatenate([real_rows, imag_rows], axis=2)


def shift_matrix(length, lags, limit):
    shape = (length, lags, length)
    z = lax.broadcasted_iota(jnp.int32, shape, 0)
    b = lax.broadcasted_iota(jnp.int32, shape, 1)
    y = lax.broadcasted_iota(jnp.int32, shape, 2)
    return ((z == y + b) & (y < limit)).astype(jnp.float32)


def realified(real_part, imag_part):
    top = jnp.concatenate([real_part, -imag_part], axis=-1)
    bottom = jnp.concatenate([imag_part, real_part], axis=-1)
    return jnp.concatenate([top, bottom], axis=-2)


def packed(real_part, imag_part):
    upper = lax.broadcasted_iota(jnp.int32, real_part.shape, real_part.ndim - 2) <= lax.broadcasted_iota(
        jnp.int32, real_part.shape, real_part.ndim - 1
    )
    return jnp.where(upper, real_part, imag_part)


def unpacked(square):
    row_id = lax.broadcasted_iota(jnp.int32, square.shape, square.ndim - 2)
    col_id = lax.broadcasted_iota(jnp.int32, square.shape, square.ndim - 1)
    mirrored = jnp.swapaxes(square, -1, -2)
    real_part = jnp.where(row_id <= col_id, square, mirrored)
    imag_part = jnp.where(row_id > col_id, square, jnp.where(row_id == col_id, 0.0, -mirrored))
    return real_part, imag_part


def inverse_factor(left):
    count, width = left.shape
    half = width // 2
    row_id = lax.broadcasted_iota(jnp.int32, left.shape, 0)
    lane_id = lax.broadcasted_iota(jnp.int32, left.shape, 1)
    sign = jnp.where(lane_id[:1] < half, -1.0, 1.0)
    rows_only = row_id[:, :1]

    def body(k, carry):
        left, inverse, pivots = carry
        at_row = row_id == k
        col_real = jnp.sum(jnp.where(lane_id == k, left, 0.0), axis=1, keepdims=True)
        col_imag = jnp.sum(jnp.where(lane_id == k + half, left, 0.0), axis=1, keepdims=True)
        row_left = jnp.sum(jnp.where(at_row, left, 0.0), axis=0, keepdims=True)
        row_inverse = jnp.sum(jnp.where(at_row, inverse, 0.0), axis=0, keepdims=True)
        pivot = jnp.sum(jnp.where(rows_only == k, col_real, 0.0), axis=0, keepdims=True)
        scale = 1.0 / pivot
        below = rows_only > k
        by_real = jnp.where(below, col_real, 0.0) * scale
        by_imag = jnp.where(below, col_imag, 0.0) * scale
        left = left - (by_real * row_left + by_imag * (pltpu.roll(row_left, half, 1) * sign))
        inverse = inverse - (
            by_real * row_inverse + by_imag * (pltpu.roll(row_inverse, half, 1) * sign)
        )
        pivots = jnp.where(rows_only == k, pivot, pivots)
        return left, inverse, pivots

    eye = (row_id == lane_id).astype(jnp.float32)
    start = (left, eye, jnp.zeros((count, 1), jnp.float32))
    _, inverse, pivots = lax.fori_loop(0, count, body, start)
    return inverse * lax.rsqrt(pivots)


def turned(rows):
    width = rows.shape[1] // 2
    return jnp.concatenate([-rows[:, width:], rows[:, :width]], axis=1)


def dot(left, right):
    return jnp.dot(left, right, precision=exact_mode, preferred_element_type=jnp.float32)


def power_kernel(cov_ref, start_ref, out_ref):
    square = cov_ref[0]
    mirrored = square.T
    row_id = lax.broadcasted_iota(jnp.int32, square.shape, 0)
    col_id = lax.broadcasted_iota(jnp.int32, square.shape, 1)
    cov_real = jnp.where(row_id <= col_id, square, mirrored)
    cov_imag = jnp.where(row_id > col_id, square, jnp.where(row_id == col_id, 0.0, -mirrored))
    half = start_ref.shape[1] // 2
    width = square.shape[0]
    subspace = start_ref[0, :half, :]
    pad = jnp.zeros((64 - half, 2 * width), jnp.float32)
    contract = (((1,), (1,)), ((), ()))
    for power_step in range(POWER):
        sub_real = subspace[:, :width]
        sub_imag = subspace[:, width:]
        summed = jnp.concatenate(
            [
                dot(sub_real, cov_real) + dot(sub_imag, cov_imag),
                dot(sub_imag, cov_real) - dot(sub_real, cov_imag),
            ],
            axis=1,
        )
        stacked = jnp.concatenate([summed, pad, turned(summed), pad], axis=0)
        gram_matrix = lax.dot_general(
            summed, stacked, contract, precision=exact_mode, preferred_element_type=jnp.float32
        )
        subspace = dot(inverse_factor(gram_matrix), stacked)
    out_ref[0, :half, :] = subspace
    out_ref[0, half:, :] = turned(subspace)


def power_steps(cov_square, subspace):
    freq_count, basis, width = subspace.shape
    rows = cov_square.shape[1]
    return pl.pallas_call(
        power_kernel,
        out_shape=jax.ShapeDtypeStruct(subspace.shape, jnp.float32),
        grid=(freq_count,),
        in_specs=[
            pl.BlockSpec((1, rows, rows), lambda i: (i, 0, 0)),
            pl.BlockSpec((1, basis, width), lambda i: (i, 0, 0)),
        ],
        out_specs=pl.BlockSpec((1, basis, width), lambda i: (i, 0, 0)),
    )(cov_square, subspace)


def counts_along(places, lags, limit):
    total = jnp.zeros(places.shape, jnp.float32)
    for shift_by in range(lags):
        inside = (places - shift_by >= 0) & (places - shift_by < limit)
        total = total + inside.astype(jnp.float32)
    return total


def on_device(traces, kept_bins, start_basis):
    space_count = lax.axis_size("space")
    cosines, sines = tables(kept_bins)
    dft_scale = 1.0 / math.sqrt(NT)
    waves = jnp.stack([cosines * dft_scale, -sines * dft_scale], axis=1)
    spectra_tile = product("xyt,tcf->fcxy", traces, waves)
    slices = lax.all_to_all(spectra_tile, "freq", split_axis=0, concat_axis=3, tiled=True)
    freq_count = slices.shape[0]
    strip_width = slices.shape[2]
    trace_cols = slices.shape[3]
    rows = LX * LY
    x_offset = lax.axis_index("space") * strip_width
    places = x_offset + jnp.arange(strip_width, dtype=jnp.int32)
    columns = jnp.arange(trace_cols, dtype=jnp.int32)
    limit_x = strip_width * space_count - LX + 1
    limit_y = trace_cols - LY + 1
    valid_x = (places < limit_x).astype(jnp.float32)
    counts = (
        counts_along(places, LX, limit_x)[:, None] * counts_along(columns, LY, limit_y)[None, :]
    )
    lag_shift = shift_matrix(trace_cols, LY, limit_y)
    subspace = paired(start_basis)
    next_counts = (
        counts_along(places + strip_width, LX, limit_x)[:, None]
        * counts_along(columns, LY, limit_y)[None, :]
    )[: LX - 1]
    next_counts = jnp.maximum(next_counts, 1.0)
    rim_rows = shifted(slices[:, :, : LX - 1, :], "space", -1)
    for cadzow_step in range(CADZOW):
        extended = jnp.concatenate([slices, rim_rows], axis=2)
        lagged = product("fcpz,zby->fcbpy", extended, lag_shift)
        matrix = jnp.stack(
            [lagged[:, :, :, lag_x : lag_x + strip_width, :] for lag_x in range(LX)], axis=2
        )
        matrix = matrix * valid_x[:, None]
        matrix = matrix.reshape(freq_count, 2 * rows, strip_width * trace_cols)
        gram_h = product("fik,fjk->fij", matrix, matrix, lax.Precision.HIGH)
        cov_real = gram_h[:, :rows, :rows] + gram_h[:, rows:, rows:]
        cov_imag = gram_h[:, rows:, :rows] - gram_h[:, :rows, rows:]
        cov = all_sum(packed(cov_real, cov_imag), "space")
        subspace = power_steps(cov, subspace)
        half = subspace.shape[1] // 2
        signs = jnp.where(jnp.arange(2 * half) < half, 1.0, -1.0)[:, None]
        weights = subspace * signs
        coeffs = product("fjk,fkc->fjc", weights, matrix, lax.Precision.HIGH)
        projected = product("fjk,fjc->fkc", weights, coeffs, lax.Precision.HIGH)
        projected = projected.reshape(freq_count, 2, LX, LY, strip_width, trace_cols)
        along_y = product("fcabxy,vby->fcaxv", projected, lag_shift)
        full = sum(
            jnp.pad(along_y[:, :, lag_x], ((0, 0), (0, 0), (lag_x, LX - 1 - lag_x), (0, 0)))
            for lag_x in range(LX)
        )
        tail = full[:, :, strip_width:, :]
        spill = shifted(tail, "space", 1)
        if cadzow_step + 1 < CADZOW:
            next_head = shifted(full[:, :, : LX - 1, :], "space", -1)
            rim_rows = (next_head + tail) / next_counts
        spill = jnp.pad(spill, ((0, 0), (0, 0), (0, strip_width - (LX - 1)), (0, 0)))
        slices = (full[:, :, :strip_width, :] + spill) / counts
    out_scale = math.sqrt(2.0 / kept_bins.shape[0])
    received = lax.all_to_all(slices, "freq", split_axis=3, concat_axis=0, tiled=True)
    synth = product("fxy,tf->xyt", received[:, 0], cosines)
    synth = synth - product("fxy,tf->xyt", received[:, 1], sines)
    return out_scale * synth


def solution(mesh):
    placed = (P("space", "freq", None), P(), P("freq", None, None, None))
    return jax.shard_map(
        on_device, mesh=mesh, in_specs=placed, out_specs=P("space", "freq", None), check_vma=False
    )
```

```python
import math

import jax
import jax.numpy as jnp
from jax import lax
from jax.experimental import pallas as pl
from jax.experimental.pallas import tpu as pltpu
from jax.sharding import PartitionSpec as P

NT = 2048
LX = 8
LY = 32
RANK = 40
POWER = 4
CADZOW = 2


exact_mode = lax.Precision.HIGHEST


def shifted(x, axis, by):
    count = lax.axis_size(axis)
    pairs = [(i, i + by) for i in range(count) if 0 <= i + by < count]
    return lax.ppermute(x, axis, pairs)


def all_sum(x, axis):
    count = lax.axis_size(axis)
    chunks = x.reshape(count, -1)
    mine = lax.all_to_all(chunks, axis, 0, 0, tiled=True).sum(axis=0)
    copies = jnp.broadcast_to(mine[None], (count, mine.shape[0]))
    return lax.all_to_all(copies, axis, 0, 0, tiled=True).reshape(x.shape)


def product(form, left, right, precision=exact_mode):
    return jnp.einsum(form, left, right, precision=precision, preferred_element_type=jnp.float32)


def tables(kept_bins):
    samples = jnp.arange(NT, dtype=jnp.int32)
    phases = samples[:, None] * kept_bins[None, :] % NT
    angles = phases.astype(jnp.float32) * (2.0 * math.pi / NT)
    return (jnp.cos(angles), jnp.sin(angles))


def paired(start):
    real_rows = jnp.concatenate([start[:, 0], -start[:, 1]], axis=1)
    imag_rows = jnp.concatenate([start[:, 1], start[:, 0]], axis=1)
    return jnp.concatenate([real_rows, imag_rows], axis=2)


def shift_matrix(length, lags, limit):
    shape = (length, lags, length)
    z = lax.broadcasted_iota(jnp.int32, shape, 0)
    b = lax.broadcasted_iota(jnp.int32, shape, 1)
    y = lax.broadcasted_iota(jnp.int32, shape, 2)
    return ((z == y + b) & (y < limit)).astype(jnp.float32)


def realified(real_part, imag_part):
    top = jnp.concatenate([real_part, -imag_part], axis=-1)
    bottom = jnp.concatenate([imag_part, real_part], axis=-1)
    return jnp.concatenate([top, bottom], axis=-2)


def packed(real_part, imag_part):
    upper = lax.broadcasted_iota(jnp.int32, real_part.shape, real_part.ndim - 2) <= lax.broadcasted_iota(
        jnp.int32, real_part.shape, real_part.ndim - 1
    )
    return jnp.where(upper, real_part, imag_part)


def unpacked(square):
    row_id = lax.broadcasted_iota(jnp.int32, square.shape, square.ndim - 2)
    col_id = lax.broadcasted_iota(jnp.int32, square.shape, square.ndim - 1)
    mirrored = jnp.swapaxes(square, -1, -2)
    real_part = jnp.where(row_id <= col_id, square, mirrored)
    imag_part = jnp.where(row_id > col_id, square, jnp.where(row_id == col_id, 0.0, -mirrored))
    return real_part, imag_part


def inverse_factor(left):
    count, width = left.shape
    half = width // 2
    row_id = lax.broadcasted_iota(jnp.int32, left.shape, 0)
    lane_id = lax.broadcasted_iota(jnp.int32, left.shape, 1)
    sign = jnp.where(lane_id[:1] < half, -1.0, 1.0)
    rows_only = row_id[:, :1]

    def body(k, carry):
        left, inverse, pivots = carry
        at_row = row_id == k
        col_real = jnp.sum(jnp.where(lane_id == k, left, 0.0), axis=1, keepdims=True)
        col_imag = jnp.sum(jnp.where(lane_id == k + half, left, 0.0), axis=1, keepdims=True)
        row_left = jnp.sum(jnp.where(at_row, left, 0.0), axis=0, keepdims=True)
        row_inverse = jnp.sum(jnp.where(at_row, inverse, 0.0), axis=0, keepdims=True)
        pivot = jnp.sum(jnp.where(rows_only == k, col_real, 0.0), axis=0, keepdims=True)
        scale = 1.0 / pivot
        below = rows_only > k
        by_real = jnp.where(below, col_real, 0.0) * scale
        by_imag = jnp.where(below, col_imag, 0.0) * scale
        left = left - (by_real * row_left + by_imag * (pltpu.roll(row_left, half, 1) * sign))
        inverse = inverse - (
            by_real * row_inverse + by_imag * (pltpu.roll(row_inverse, half, 1) * sign)
        )
        pivots = jnp.where(rows_only == k, pivot, pivots)
        return left, inverse, pivots

    eye = (row_id == lane_id).astype(jnp.float32)
    start = (left, eye, jnp.zeros((count, 1), jnp.float32))
    _, inverse, pivots = lax.fori_loop(0, count, body, start)
    return inverse * lax.rsqrt(pivots)


def turned(rows):
    width = rows.shape[1] // 2
    return jnp.concatenate([-rows[:, width:], rows[:, :width]], axis=1)


def dot(left, right):
    return jnp.dot(left, right, precision=exact_mode, preferred_element_type=jnp.float32)


def power_kernel(cov_ref, start_ref, out_ref):
    square = cov_ref[0]
    mirrored = square.T
    row_id = lax.broadcasted_iota(jnp.int32, square.shape, 0)
    col_id = lax.broadcasted_iota(jnp.int32, square.shape, 1)
    cov_real = jnp.where(row_id <= col_id, square, mirrored)
    cov_imag = jnp.where(row_id > col_id, square, jnp.where(row_id == col_id, 0.0, -mirrored))
    half = start_ref.shape[1] // 2
    width = square.shape[0]
    subspace = start_ref[0, :half, :]
    pad = jnp.zeros((64 - half, 2 * width), jnp.float32)
    contract = (((1,), (1,)), ((), ()))
    for power_step in range(POWER):
        sub_real = subspace[:, :width]
        sub_imag = subspace[:, width:]
        summed = jnp.concatenate(
            [
                dot(sub_real, cov_real) + dot(sub_imag, cov_imag),
                dot(sub_imag, cov_real) - dot(sub_real, cov_imag),
            ],
            axis=1,
        )
        stacked = jnp.concatenate([summed, pad, turned(summed), pad], axis=0)
        gram_matrix = lax.dot_general(
            summed, stacked, contract, precision=exact_mode, preferred_element_type=jnp.float32
        )
        subspace = dot(inverse_factor(gram_matrix), stacked)
    out_ref[0, :half, :] = subspace
    out_ref[0, half:, :] = turned(subspace)


def power_steps(cov_square, subspace):
    freq_count, basis, width = subspace.shape
    rows = cov_square.shape[1]
    return pl.pallas_call(
        power_kernel,
        out_shape=jax.ShapeDtypeStruct(subspace.shape, jnp.float32),
        grid=(freq_count,),
        in_specs=[
            pl.BlockSpec((1, rows, rows), lambda i: (i, 0, 0)),
            pl.BlockSpec((1, basis, width), lambda i: (i, 0, 0)),
        ],
        out_specs=pl.BlockSpec((1, basis, width), lambda i: (i, 0, 0)),
    )(cov_square, subspace)


def counts_along(places, lags, limit):
    total = jnp.zeros(places.shape, jnp.float32)
    for shift_by in range(lags):
        inside = (places - shift_by >= 0) & (places - shift_by < limit)
        total = total + inside.astype(jnp.float32)
    return total


def on_device(traces, kept_bins, start_basis):
    space_count = lax.axis_size("space")
    cosines, sines = tables(kept_bins)
    dft_scale = 1.0 / math.sqrt(NT)
    waves = jnp.stack([cosines * dft_scale, -sines * dft_scale], axis=1)
    spectra_tile = product("xyt,tcf->fcxy", traces, waves)
    slices = lax.all_to_all(spectra_tile, "freq", split_axis=0, concat_axis=3, tiled=True)
    freq_count = slices.shape[0]
    strip_width = slices.shape[2]
    trace_cols = slices.shape[3]
    rows = LX * LY
    x_offset = lax.axis_index("space") * strip_width
    places = x_offset + jnp.arange(strip_width, dtype=jnp.int32)
    columns = jnp.arange(trace_cols, dtype=jnp.int32)
    limit_x = strip_width * space_count - LX + 1
    limit_y = trace_cols - LY + 1
    valid_x = (places < limit_x).astype(jnp.float32)
    counts = (
        counts_along(places, LX, limit_x)[:, None] * counts_along(columns, LY, limit_y)[None, :]
    )
    lag_shift = shift_matrix(trace_cols, LY, limit_y)
    subspace = paired(start_basis)
    next_counts = (
        counts_along(places + strip_width, LX, limit_x)[:, None]
        * counts_along(columns, LY, limit_y)[None, :]
    )[: LX - 1]
    next_counts = jnp.maximum(next_counts, 1.0)
    rim_rows = shifted(slices[:, :, : LX - 1, :], "space", -1)
    for cadzow_step in range(CADZOW):
        extended = jnp.concatenate([slices, rim_rows], axis=2)
        lagged = product("fcpz,zby->fcbpy", extended, lag_shift)
        matrix = jnp.stack(
            [lagged[:, :, :, lag_x : lag_x + strip_width, :] for lag_x in range(LX)], axis=2
        )
        matrix = matrix * valid_x[:, None]
        matrix = matrix.reshape(freq_count, 2 * rows, strip_width * trace_cols)
        gram_h = product("fik,fjk->fij", matrix, matrix)
        cov_real = gram_h[:, :rows, :rows] + gram_h[:, rows:, rows:]
        cov_imag = gram_h[:, rows:, :rows] - gram_h[:, :rows, rows:]
        cov = all_sum(packed(cov_real, cov_imag), "space")
        subspace = power_steps(cov, subspace)
        half = subspace.shape[1] // 2
        signs = jnp.where(jnp.arange(2 * half) < half, 1.0, -1.0)[:, None]
        weights = subspace * signs
        coeffs = product("fjk,fkc->fjc", weights, matrix, lax.Precision.HIGH)
        projected = product("fjk,fjc->fkc", weights, coeffs, lax.Precision.HIGH)
        projected = projected.reshape(freq_count, 2, LX, LY, strip_width, trace_cols)
        along_y = product("fcabxy,vby->fcaxv", projected, lag_shift)
        full = sum(
            jnp.pad(along_y[:, :, lag_x], ((0, 0), (0, 0), (lag_x, LX - 1 - lag_x), (0, 0)))
            for lag_x in range(LX)
        )
        tail = full[:, :, strip_width:, :]
        spill = shifted(tail, "space", 1)
        if cadzow_step + 1 < CADZOW:
            next_head = shifted(full[:, :, : LX - 1, :], "space", -1)
            rim_rows = (next_head + tail) / next_counts
        spill = jnp.pad(spill, ((0, 0), (0, 0), (0, strip_width - (LX - 1)), (0, 0)))
        slices = (full[:, :, :strip_width, :] + spill) / counts
    out_scale = math.sqrt(2.0 / kept_bins.shape[0])
    received = lax.all_to_all(slices, "freq", split_axis=3, concat_axis=0, tiled=True)
    synth = product("fxy,tf->xyt", received[:, 0], cosines)
    synth = synth - product("fxy,tf->xyt", received[:, 1], sines)
    return out_scale * synth


def solution(mesh):
    placed = (P("space", "freq", None), P(), P("freq", None, None, None))
    return jax.shard_map(
        on_device, mesh=mesh, in_specs=placed, out_specs=P("space", "freq", None), check_vma=False
    )
```

```python
import math

import jax
import jax.numpy as jnp
from jax import lax
from jax.experimental import pallas as pl
from jax.experimental.pallas import tpu as pltpu
from jax.sharding import PartitionSpec as P

NT = 2048
LX = 8
LY = 32
RANK = 40
POWER = 4
CADZOW = 2


exact_mode = lax.Precision.HIGHEST


def shifted(x, axis, by):
    count = lax.axis_size(axis)
    pairs = [(i, i + by) for i in range(count) if 0 <= i + by < count]
    return lax.ppermute(x, axis, pairs)


def all_sum(x, axis):
    count = lax.axis_size(axis)
    chunks = x.reshape(count, -1)
    mine = lax.all_to_all(chunks, axis, 0, 0, tiled=True).sum(axis=0)
    copies = jnp.broadcast_to(mine[None], (count, mine.shape[0]))
    return lax.all_to_all(copies, axis, 0, 0, tiled=True).reshape(x.shape)


def product(form, left, right, precision=exact_mode):
    return jnp.einsum(form, left, right, precision=precision, preferred_element_type=jnp.float32)


def tables(kept_bins):
    samples = jnp.arange(NT, dtype=jnp.int32)
    phases = samples[:, None] * kept_bins[None, :] % NT
    angles = phases.astype(jnp.float32) * (2.0 * math.pi / NT)
    return (jnp.cos(angles), jnp.sin(angles))


def paired(start):
    real_rows = jnp.concatenate([start[:, 0], -start[:, 1]], axis=1)
    imag_rows = jnp.concatenate([start[:, 1], start[:, 0]], axis=1)
    return jnp.concatenate([real_rows, imag_rows], axis=2)


def shift_matrix(length, lags, limit):
    shape = (length, lags, length)
    z = lax.broadcasted_iota(jnp.int32, shape, 0)
    b = lax.broadcasted_iota(jnp.int32, shape, 1)
    y = lax.broadcasted_iota(jnp.int32, shape, 2)
    return ((z == y + b) & (y < limit)).astype(jnp.float32)


def realified(real_part, imag_part):
    top = jnp.concatenate([real_part, -imag_part], axis=-1)
    bottom = jnp.concatenate([imag_part, real_part], axis=-1)
    return jnp.concatenate([top, bottom], axis=-2)


def packed(real_part, imag_part):
    upper = lax.broadcasted_iota(jnp.int32, real_part.shape, real_part.ndim - 2) <= lax.broadcasted_iota(
        jnp.int32, real_part.shape, real_part.ndim - 1
    )
    return jnp.where(upper, real_part, imag_part)


def unpacked(square):
    row_id = lax.broadcasted_iota(jnp.int32, square.shape, square.ndim - 2)
    col_id = lax.broadcasted_iota(jnp.int32, square.shape, square.ndim - 1)
    mirrored = jnp.swapaxes(square, -1, -2)
    real_part = jnp.where(row_id <= col_id, square, mirrored)
    imag_part = jnp.where(row_id > col_id, square, jnp.where(row_id == col_id, 0.0, -mirrored))
    return real_part, imag_part


def inverse_factor(left):
    count, width = left.shape
    half = width // 2
    row_id = lax.broadcasted_iota(jnp.int32, left.shape, 0)
    lane_id = lax.broadcasted_iota(jnp.int32, left.shape, 1)
    sign = jnp.where(lane_id[:1] < half, -1.0, 1.0)
    rows_only = row_id[:, :1]

    def body(k, carry):
        left, inverse, pivots = carry
        at_row = row_id == k
        col_real = jnp.sum(jnp.where(lane_id == k, left, 0.0), axis=1, keepdims=True)
        col_imag = jnp.sum(jnp.where(lane_id == k + half, left, 0.0), axis=1, keepdims=True)
        row_left = jnp.sum(jnp.where(at_row, left, 0.0), axis=0, keepdims=True)
        row_inverse = jnp.sum(jnp.where(at_row, inverse, 0.0), axis=0, keepdims=True)
        pivot = jnp.sum(jnp.where(rows_only == k, col_real, 0.0), axis=0, keepdims=True)
        scale = 1.0 / pivot
        below = rows_only > k
        by_real = jnp.where(below, col_real, 0.0) * scale
        by_imag = jnp.where(below, col_imag, 0.0) * scale
        left = left - (by_real * row_left + by_imag * (pltpu.roll(row_left, half, 1) * sign))
        inverse = inverse - (
            by_real * row_inverse + by_imag * (pltpu.roll(row_inverse, half, 1) * sign)
        )
        pivots = jnp.where(rows_only == k, pivot, pivots)
        return left, inverse, pivots

    eye = (row_id == lane_id).astype(jnp.float32)
    start = (left, eye, jnp.zeros((count, 1), jnp.float32))
    _, inverse, pivots = lax.fori_loop(0, count, body, start, unroll=4)
    return inverse * lax.rsqrt(pivots)


def turned(rows):
    width = rows.shape[1] // 2
    return jnp.concatenate([-rows[:, width:], rows[:, :width]], axis=1)


def dot(left, right):
    return jnp.dot(left, right, precision=exact_mode, preferred_element_type=jnp.float32)


def power_kernel(cov_ref, start_ref, out_ref):
    square = cov_ref[0]
    mirrored = square.T
    row_id = lax.broadcasted_iota(jnp.int32, square.shape, 0)
    col_id = lax.broadcasted_iota(jnp.int32, square.shape, 1)
    cov_real = jnp.where(row_id <= col_id, square, mirrored)
    cov_imag = jnp.where(row_id > col_id, square, jnp.where(row_id == col_id, 0.0, -mirrored))
    half = start_ref.shape[1] // 2
    width = square.shape[0]
    subspace = start_ref[0, :half, :]
    pad = jnp.zeros((64 - half, 2 * width), jnp.float32)
    contract = (((1,), (1,)), ((), ()))
    for power_step in range(POWER):
        sub_real = subspace[:, :width]
        sub_imag = subspace[:, width:]
        summed = jnp.concatenate(
            [
                dot(sub_real, cov_real) + dot(sub_imag, cov_imag),
                dot(sub_imag, cov_real) - dot(sub_real, cov_imag),
            ],
            axis=1,
        )
        stacked = jnp.concatenate([summed, pad, turned(summed), pad], axis=0)
        gram_matrix = lax.dot_general(
            summed, stacked, contract, precision=exact_mode, preferred_element_type=jnp.float32
        )
        subspace = dot(inverse_factor(gram_matrix), stacked)
    out_ref[0, :half, :] = subspace
    out_ref[0, half:, :] = turned(subspace)


def power_steps(cov_square, subspace):
    freq_count, basis, width = subspace.shape
    rows = cov_square.shape[1]
    return pl.pallas_call(
        power_kernel,
        out_shape=jax.ShapeDtypeStruct(subspace.shape, jnp.float32),
        grid=(freq_count,),
        in_specs=[
            pl.BlockSpec((1, rows, rows), lambda i: (i, 0, 0)),
            pl.BlockSpec((1, basis, width), lambda i: (i, 0, 0)),
        ],
        out_specs=pl.BlockSpec((1, basis, width), lambda i: (i, 0, 0)),
    )(cov_square, subspace)


def counts_along(places, lags, limit):
    total = jnp.zeros(places.shape, jnp.float32)
    for shift_by in range(lags):
        inside = (places - shift_by >= 0) & (places - shift_by < limit)
        total = total + inside.astype(jnp.float32)
    return total


def on_device(traces, kept_bins, start_basis):
    space_count = lax.axis_size("space")
    cosines, sines = tables(kept_bins)
    dft_scale = 1.0 / math.sqrt(NT)
    waves = jnp.stack([cosines * dft_scale, -sines * dft_scale], axis=1)
    spectra_tile = product("xyt,tcf->fcxy", traces, waves)
    slices = lax.all_to_all(spectra_tile, "freq", split_axis=0, concat_axis=3, tiled=True)
    freq_count = slices.shape[0]
    strip_width = slices.shape[2]
    trace_cols = slices.shape[3]
    rows = LX * LY
    x_offset = lax.axis_index("space") * strip_width
    places = x_offset + jnp.arange(strip_width, dtype=jnp.int32)
    columns = jnp.arange(trace_cols, dtype=jnp.int32)
    limit_x = strip_width * space_count - LX + 1
    limit_y = trace_cols - LY + 1
    valid_x = (places < limit_x).astype(jnp.float32)
    counts = (
        counts_along(places, LX, limit_x)[:, None] * counts_along(columns, LY, limit_y)[None, :]
    )
    lag_shift = shift_matrix(trace_cols, LY, limit_y)
    subspace = paired(start_basis)
    next_counts = (
        counts_along(places + strip_width, LX, limit_x)[:, None]
        * counts_along(columns, LY, limit_y)[None, :]
    )[: LX - 1]
    next_counts = jnp.maximum(next_counts, 1.0)
    rim_rows = shifted(slices[:, :, : LX - 1, :], "space", -1)
    for cadzow_step in range(CADZOW):
        extended = jnp.concatenate([slices, rim_rows], axis=2)
        lagged = product("fcpz,zby->fcbpy", extended, lag_shift)
        matrix = jnp.stack(
            [lagged[:, :, :, lag_x : lag_x + strip_width, :] for lag_x in range(LX)], axis=2
        )
        matrix = matrix * valid_x[:, None]
        matrix = matrix.reshape(freq_count, 2 * rows, strip_width * trace_cols)
        gram_h = product("fik,fjk->fij", matrix, matrix, lax.Precision.HIGH)
        cov_real = gram_h[:, :rows, :rows] + gram_h[:, rows:, rows:]
        cov_imag = gram_h[:, rows:, :rows] - gram_h[:, :rows, rows:]
        cov = all_sum(packed(cov_real, cov_imag), "space")
        subspace = power_steps(cov, subspace)
        half = subspace.shape[1] // 2
        signs = jnp.where(jnp.arange(2 * half) < half, 1.0, -1.0)[:, None]
        weights = subspace * signs
        coeffs = product("fjk,fkc->fjc", weights, matrix, lax.Precision.HIGH)
        projected = product("fjk,fjc->fkc", weights, coeffs, lax.Precision.HIGH)
        projected = projected.reshape(freq_count, 2, LX, LY, strip_width, trace_cols)
        along_y = product("fcabxy,vby->fcaxv", projected, lag_shift)
        full = sum(
            jnp.pad(along_y[:, :, lag_x], ((0, 0), (0, 0), (lag_x, LX - 1 - lag_x), (0, 0)))
            for lag_x in range(LX)
        )
        tail = full[:, :, strip_width:, :]
        spill = shifted(tail, "space", 1)
        if cadzow_step + 1 < CADZOW:
            next_head = shifted(full[:, :, : LX - 1, :], "space", -1)
            rim_rows = (next_head + tail) / next_counts
        spill = jnp.pad(spill, ((0, 0), (0, 0), (0, strip_width - (LX - 1)), (0, 0)))
        slices = (full[:, :, :strip_width, :] + spill) / counts
    out_scale = math.sqrt(2.0 / kept_bins.shape[0])
    received = lax.all_to_all(slices, "freq", split_axis=3, concat_axis=0, tiled=True)
    synth = product("fxy,tf->xyt", received[:, 0], cosines)
    synth = synth - product("fxy,tf->xyt", received[:, 1], sines)
    return out_scale * synth


def solution(mesh):
    placed = (P("space", "freq", None), P(), P("freq", None, None, None))
    return jax.shard_map(
        on_device, mesh=mesh, in_specs=placed, out_specs=P("space", "freq", None), check_vma=False
    )
```

```python
import math

import jax
import jax.numpy as jnp
from jax import lax
from jax.experimental import pallas as pl
from jax.experimental.pallas import tpu as pltpu
from jax.sharding import PartitionSpec as P

NT = 2048
LX = 8
LY = 32
RANK = 40
POWER = 4
CADZOW = 2


exact_mode = lax.Precision.HIGHEST


def shifted(x, axis, by):
    count = lax.axis_size(axis)
    pairs = [(i, i + by) for i in range(count) if 0 <= i + by < count]
    return lax.ppermute(x, axis, pairs)


def all_sum(x, axis):
    count = lax.axis_size(axis)
    chunks = x.reshape(count, -1)
    mine = lax.all_to_all(chunks, axis, 0, 0, tiled=True).sum(axis=0)
    copies = jnp.broadcast_to(mine[None], (count, mine.shape[0]))
    return lax.all_to_all(copies, axis, 0, 0, tiled=True).reshape(x.shape)


def product(form, left, right, precision=exact_mode):
    return jnp.einsum(form, left, right, precision=precision, preferred_element_type=jnp.float32)


def tables(kept_bins):
    samples = jnp.arange(NT, dtype=jnp.int32)
    phases = samples[:, None] * kept_bins[None, :] % NT
    angles = phases.astype(jnp.float32) * (2.0 * math.pi / NT)
    return (jnp.cos(angles), jnp.sin(angles))


def paired(start):
    real_rows = jnp.concatenate([start[:, 0], -start[:, 1]], axis=1)
    imag_rows = jnp.concatenate([start[:, 1], start[:, 0]], axis=1)
    return jnp.concatenate([real_rows, imag_rows], axis=2)


def shift_matrix(length, lags, limit):
    shape = (length, lags, length)
    z = lax.broadcasted_iota(jnp.int32, shape, 0)
    b = lax.broadcasted_iota(jnp.int32, shape, 1)
    y = lax.broadcasted_iota(jnp.int32, shape, 2)
    return ((z == y + b) & (y < limit)).astype(jnp.float32)


def realified(real_part, imag_part):
    top = jnp.concatenate([real_part, -imag_part], axis=-1)
    bottom = jnp.concatenate([imag_part, real_part], axis=-1)
    return jnp.concatenate([top, bottom], axis=-2)


def packed(real_part, imag_part):
    upper = lax.broadcasted_iota(jnp.int32, real_part.shape, real_part.ndim - 2) <= lax.broadcasted_iota(
        jnp.int32, real_part.shape, real_part.ndim - 1
    )
    return jnp.where(upper, real_part, imag_part)


def unpacked(square):
    row_id = lax.broadcasted_iota(jnp.int32, square.shape, square.ndim - 2)
    col_id = lax.broadcasted_iota(jnp.int32, square.shape, square.ndim - 1)
    mirrored = jnp.swapaxes(square, -1, -2)
    real_part = jnp.where(row_id <= col_id, square, mirrored)
    imag_part = jnp.where(row_id > col_id, square, jnp.where(row_id == col_id, 0.0, -mirrored))
    return real_part, imag_part


def inverse_factor(left):
    count, width = left.shape
    half = width // 2
    row_id = lax.broadcasted_iota(jnp.int32, left.shape, 0)
    lane_id = lax.broadcasted_iota(jnp.int32, left.shape, 1)
    sign = jnp.where(lane_id[:1] < half, -1.0, 1.0)
    rows_only = row_id[:, :1]

    def body(k, carry):
        left, inverse, pivots = carry
        at_row = row_id == k
        col_real = jnp.sum(jnp.where(lane_id == k, left, 0.0), axis=1, keepdims=True)
        col_imag = jnp.sum(jnp.where(lane_id == k + half, left, 0.0), axis=1, keepdims=True)
        row_left = jnp.sum(jnp.where(at_row, left, 0.0), axis=0, keepdims=True)
        row_inverse = jnp.sum(jnp.where(at_row, inverse, 0.0), axis=0, keepdims=True)
        pivot = jnp.sum(jnp.where(rows_only == k, col_real, 0.0), axis=0, keepdims=True)
        scale = 1.0 / pivot
        below = rows_only > k
        by_real = jnp.where(below, col_real, 0.0) * scale
        by_imag = jnp.where(below, col_imag, 0.0) * scale
        left = left - (by_real * row_left + by_imag * (pltpu.roll(row_left, half, 1) * sign))
        inverse = inverse - (
            by_real * row_inverse + by_imag * (pltpu.roll(row_inverse, half, 1) * sign)
        )
        pivots = jnp.where(rows_only == k, pivot, pivots)
        return left, inverse, pivots

    eye = (row_id == lane_id).astype(jnp.float32)
    start = (left, eye, jnp.zeros((count, 1), jnp.float32))
    _, inverse, pivots = lax.fori_loop(0, count, body, start, unroll=4)
    return inverse * lax.rsqrt(pivots)


def turned(rows):
    width = rows.shape[1] // 2
    return jnp.concatenate([-rows[:, width:], rows[:, :width]], axis=1)


def dot(left, right):
    return jnp.dot(left, right, precision=exact_mode, preferred_element_type=jnp.float32)


def power_kernel(cov_ref, start_ref, out_ref):
    square = cov_ref[0]
    mirrored = square.T
    row_id = lax.broadcasted_iota(jnp.int32, square.shape, 0)
    col_id = lax.broadcasted_iota(jnp.int32, square.shape, 1)
    cov_real = jnp.where(row_id <= col_id, square, mirrored)
    cov_imag = jnp.where(row_id > col_id, square, jnp.where(row_id == col_id, 0.0, -mirrored))
    half = start_ref.shape[1] // 2
    width = square.shape[0]
    subspace = start_ref[0, :half, :]
    pad = jnp.zeros((64 - half, 2 * width), jnp.float32)
    contract = (((1,), (1,)), ((), ()))
    for power_step in range(POWER):
        sub_real = subspace[:, :width]
        sub_imag = subspace[:, width:]
        summed = jnp.concatenate(
            [
                dot(sub_real, cov_real) + dot(sub_imag, cov_imag),
                dot(sub_imag, cov_real) - dot(sub_real, cov_imag),
            ],
            axis=1,
        )
        stacked = jnp.concatenate([summed, pad, turned(summed), pad], axis=0)
        gram_matrix = lax.dot_general(
            summed, stacked, contract, precision=exact_mode, preferred_element_type=jnp.float32
        )
        subspace = dot(inverse_factor(gram_matrix), stacked)
    out_ref[0, :half, :] = subspace
    out_ref[0, half:, :] = turned(subspace)


def power_steps(cov_square, subspace):
    freq_count, basis, width = subspace.shape
    rows = cov_square.shape[1]
    return pl.pallas_call(
        power_kernel,
        out_shape=jax.ShapeDtypeStruct(subspace.shape, jnp.float32),
        grid=(freq_count,),
        in_specs=[
            pl.BlockSpec((1, rows, rows), lambda i: (i, 0, 0)),
            pl.BlockSpec((1, basis, width), lambda i: (i, 0, 0)),
        ],
        out_specs=pl.BlockSpec((1, basis, width), lambda i: (i, 0, 0)),
    )(cov_square, subspace)


def counts_along(places, lags, limit):
    total = jnp.zeros(places.shape, jnp.float32)
    for shift_by in range(lags):
        inside = (places - shift_by >= 0) & (places - shift_by < limit)
        total = total + inside.astype(jnp.float32)
    return total


def on_device(traces, kept_bins, start_basis):
    space_count = lax.axis_size("space")
    cosines, sines = tables(kept_bins)
    dft_scale = 1.0 / math.sqrt(NT)
    waves = jnp.stack([cosines * dft_scale, -sines * dft_scale], axis=1)
    spectra_tile = product("xyt,tcf->fcxy", traces, waves)
    slices = lax.all_to_all(spectra_tile, "freq", split_axis=0, concat_axis=3, tiled=True)
    freq_count = slices.shape[0]
    strip_width = slices.shape[2]
    trace_cols = slices.shape[3]
    rows = LX * LY
    x_offset = lax.axis_index("space") * strip_width
    places = x_offset + jnp.arange(strip_width, dtype=jnp.int32)
    columns = jnp.arange(trace_cols, dtype=jnp.int32)
    limit_x = strip_width * space_count - LX + 1
    limit_y = trace_cols - LY + 1
    valid_x = (places < limit_x).astype(jnp.float32)
    counts = (
        counts_along(places, LX, limit_x)[:, None] * counts_along(columns, LY, limit_y)[None, :]
    )
    lag_shift = shift_matrix(trace_cols, LY, limit_y)
    subspace = paired(start_basis)
    next_counts = (
        counts_along(places + strip_width, LX, limit_x)[:, None]
        * counts_along(columns, LY, limit_y)[None, :]
    )[: LX - 1]
    next_counts = jnp.maximum(next_counts, 1.0)
    rim_rows = shifted(slices[:, :, : LX - 1, :], "space", -1)
    for cadzow_step in range(CADZOW):
        extended = jnp.concatenate([slices, rim_rows], axis=2)
        lagged = product("fcpz,zby->fcbpy", extended, lag_shift)
        matrix = jnp.stack(
            [lagged[:, :, :, lag_x : lag_x + strip_width, :] for lag_x in range(LX)], axis=2
        )
        matrix = matrix * valid_x[:, None]
        matrix = matrix.reshape(freq_count, 2 * rows, strip_width * trace_cols)
        gram_h = product("fik,fjk->fij", matrix, matrix, lax.Precision.HIGH)
        cov_real = gram_h[:, :rows, :rows] + gram_h[:, rows:, rows:]
        cov_imag = gram_h[:, rows:, :rows] - gram_h[:, :rows, rows:]
        cov = all_sum(packed(cov_real, cov_imag), "space")
        subspace = power_steps(cov, subspace)
        half = subspace.shape[1] // 2
        signs = jnp.where(jnp.arange(2 * half) < half, 1.0, -1.0)[:, None]
        weights = subspace * signs
        coeffs = product("fjk,fkc->fjc", weights, matrix, lax.Precision.HIGH)
        projected = product("fjk,fjc->fkc", weights, coeffs, lax.Precision.HIGH)
        projected = projected.reshape(freq_count, 2, LX, LY, strip_width, trace_cols)
        along_y = product("fcabxy,vby->fcaxv", projected, lag_shift)
        full = sum(
            jnp.pad(along_y[:, :, lag_x], ((0, 0), (0, 0), (lag_x, LX - 1 - lag_x), (0, 0)))
            for lag_x in range(LX)
        )
        tail = full[:, :, strip_width:, :]
        spill = shifted(tail, "space", 1)
        if cadzow_step + 1 < CADZOW:
            next_head = shifted(full[:, :, : LX - 1, :], "space", -1)
            rim_rows = (next_head + tail) / next_counts
        spill = jnp.pad(spill, ((0, 0), (0, 0), (0, strip_width - (LX - 1)), (0, 0)))
        slices = (full[:, :, :strip_width, :] + spill) / counts
    out_scale = math.sqrt(2.0 / kept_bins.shape[0])
    received = lax.all_to_all(slices, "freq", split_axis=3, concat_axis=0, tiled=True)
    basis_waves = jnp.stack([cosines * out_scale, -sines * out_scale], axis=1)
    return product("fcxy,tcf->xyt", received, basis_waves)


def solution(mesh):
    placed = (P("space", "freq", None), P(), P("freq", None, None, None))
    return jax.shard_map(
        on_device, mesh=mesh, in_specs=placed, out_specs=P("space", "freq", None), check_vma=False
    )
```

```python
import math

import jax
import jax.numpy as jnp
from jax import lax
from jax.experimental import pallas as pl
from jax.experimental.pallas import tpu as pltpu
from jax.sharding import PartitionSpec as P

NT = 2048
LX = 8
LY = 32
RANK = 40
POWER = 4
CADZOW = 2


exact_mode = lax.Precision.HIGHEST


def shifted(x, axis, by):
    count = lax.axis_size(axis)
    pairs = [(i, i + by) for i in range(count) if 0 <= i + by < count]
    return lax.ppermute(x, axis, pairs)


def all_sum(x, axis):
    count = lax.axis_size(axis)
    chunks = x.reshape(count, -1)
    mine = lax.all_to_all(chunks, axis, 0, 0, tiled=True).sum(axis=0)
    copies = jnp.broadcast_to(mine[None], (count, mine.shape[0]))
    return lax.all_to_all(copies, axis, 0, 0, tiled=True).reshape(x.shape)


def product(form, left, right, precision=exact_mode):
    return jnp.einsum(form, left, right, precision=precision, preferred_element_type=jnp.float32)


def tables(kept_bins):
    samples = jnp.arange(NT, dtype=jnp.int32)
    phases = samples[:, None] * kept_bins[None, :] % NT
    angles = phases.astype(jnp.float32) * (2.0 * math.pi / NT)
    return (jnp.cos(angles), jnp.sin(angles))


def paired(start):
    real_rows = jnp.concatenate([start[:, 0], -start[:, 1]], axis=1)
    imag_rows = jnp.concatenate([start[:, 1], start[:, 0]], axis=1)
    return jnp.concatenate([real_rows, imag_rows], axis=2)


def shift_matrix(length, lags, limit):
    shape = (length, lags, length)
    z = lax.broadcasted_iota(jnp.int32, shape, 0)
    b = lax.broadcasted_iota(jnp.int32, shape, 1)
    y = lax.broadcasted_iota(jnp.int32, shape, 2)
    return ((z == y + b) & (y < limit)).astype(jnp.float32)


def realified(real_part, imag_part):
    top = jnp.concatenate([real_part, -imag_part], axis=-1)
    bottom = jnp.concatenate([imag_part, real_part], axis=-1)
    return jnp.concatenate([top, bottom], axis=-2)


def packed(real_part, imag_part):
    upper = lax.broadcasted_iota(jnp.int32, real_part.shape, real_part.ndim - 2) <= lax.broadcasted_iota(
        jnp.int32, real_part.shape, real_part.ndim - 1
    )
    return jnp.where(upper, real_part, imag_part)


def unpacked(square):
    row_id = lax.broadcasted_iota(jnp.int32, square.shape, square.ndim - 2)
    col_id = lax.broadcasted_iota(jnp.int32, square.shape, square.ndim - 1)
    mirrored = jnp.swapaxes(square, -1, -2)
    real_part = jnp.where(row_id <= col_id, square, mirrored)
    imag_part = jnp.where(row_id > col_id, square, jnp.where(row_id == col_id, 0.0, -mirrored))
    return real_part, imag_part


def inverse_factor(left):
    count, width = left.shape
    half = width // 2
    row_id = lax.broadcasted_iota(jnp.int32, left.shape, 0)
    lane_id = lax.broadcasted_iota(jnp.int32, left.shape, 1)
    sign = jnp.where(lane_id[:1] < half, -1.0, 1.0)
    rows_only = row_id[:, :1]

    def body(k, carry):
        left, inverse, pivots = carry
        at_row = row_id == k
        col_real = jnp.sum(jnp.where(lane_id == k, left, 0.0), axis=1, keepdims=True)
        col_imag = jnp.sum(jnp.where(lane_id == k + half, left, 0.0), axis=1, keepdims=True)
        row_left = jnp.sum(jnp.where(at_row, left, 0.0), axis=0, keepdims=True)
        row_inverse = jnp.sum(jnp.where(at_row, inverse, 0.0), axis=0, keepdims=True)
        pivot = jnp.sum(jnp.where(rows_only == k, col_real, 0.0), axis=0, keepdims=True)
        scale = 1.0 / pivot
        below = rows_only > k
        by_real = jnp.where(below, col_real, 0.0) * scale
        by_imag = jnp.where(below, col_imag, 0.0) * scale
        left = left - (by_real * row_left + by_imag * (pltpu.roll(row_left, half, 1) * sign))
        inverse = inverse - (
            by_real * row_inverse + by_imag * (pltpu.roll(row_inverse, half, 1) * sign)
        )
        pivots = jnp.where(rows_only == k, pivot, pivots)
        return left, inverse, pivots

    eye = (row_id == lane_id).astype(jnp.float32)
    start = (left, eye, jnp.zeros((count, 1), jnp.float32))
    _, inverse, pivots = lax.fori_loop(0, count, body, start, unroll=4)
    return inverse * lax.rsqrt(pivots)


def turned(rows):
    width = rows.shape[1] // 2
    return jnp.concatenate([-rows[:, width:], rows[:, :width]], axis=1)


def dot(left, right):
    return jnp.dot(left, right, precision=exact_mode, preferred_element_type=jnp.float32)


def power_kernel(cov_ref, start_ref, out_ref):
    square = cov_ref[0]
    mirrored = square.T
    row_id = lax.broadcasted_iota(jnp.int32, square.shape, 0)
    col_id = lax.broadcasted_iota(jnp.int32, square.shape, 1)
    cov_real = jnp.where(row_id <= col_id, square, mirrored)
    cov_imag = jnp.where(row_id > col_id, square, jnp.where(row_id == col_id, 0.0, -mirrored))
    half = start_ref.shape[1] // 2
    width = square.shape[0]
    subspace = start_ref[0, :half, :]
    pad = jnp.zeros((64 - half, 2 * width), jnp.float32)
    contract = (((1,), (1,)), ((), ()))
    for power_step in range(POWER):
        sub_real = subspace[:, :width]
        sub_imag = subspace[:, width:]
        summed = jnp.concatenate(
            [
                dot(sub_real, cov_real) + dot(sub_imag, cov_imag),
                dot(sub_imag, cov_real) - dot(sub_real, cov_imag),
            ],
            axis=1,
        )
        stacked = jnp.concatenate([summed, pad, turned(summed), pad], axis=0)
        gram_matrix = lax.dot_general(
            summed, stacked, contract, precision=exact_mode, preferred_element_type=jnp.float32
        )
        subspace = dot(inverse_factor(gram_matrix), stacked)
    out_ref[0, :half, :] = subspace
    out_ref[0, half:, :] = turned(subspace)


def power_steps(cov_square, subspace):
    freq_count, basis, width = subspace.shape
    rows = cov_square.shape[1]
    return pl.pallas_call(
        power_kernel,
        out_shape=jax.ShapeDtypeStruct(subspace.shape, jnp.float32),
        grid=(freq_count,),
        in_specs=[
            pl.BlockSpec((1, rows, rows), lambda i: (i, 0, 0)),
            pl.BlockSpec((1, basis, width), lambda i: (i, 0, 0)),
        ],
        out_specs=pl.BlockSpec((1, basis, width), lambda i: (i, 0, 0)),
    )(cov_square, subspace)


def counts_along(places, lags, limit):
    total = jnp.zeros(places.shape, jnp.float32)
    for shift_by in range(lags):
        inside = (places - shift_by >= 0) & (places - shift_by < limit)
        total = total + inside.astype(jnp.float32)
    return total


def on_device(traces, kept_bins, start_basis):
    space_count = lax.axis_size("space")
    cosines, sines = tables(kept_bins)
    dft_scale = 1.0 / math.sqrt(NT)
    waves = jnp.stack([cosines * dft_scale, -sines * dft_scale], axis=1)
    spectra_tile = product("xyt,tcf->fcxy", traces, waves)
    slices = lax.all_to_all(spectra_tile, "freq", split_axis=0, concat_axis=3, tiled=True)
    freq_count = slices.shape[0]
    strip_width = slices.shape[2]
    trace_cols = slices.shape[3]
    rows = LX * LY
    x_offset = lax.axis_index("space") * strip_width
    places = x_offset + jnp.arange(strip_width, dtype=jnp.int32)
    columns = jnp.arange(trace_cols, dtype=jnp.int32)
    limit_x = strip_width * space_count - LX + 1
    limit_y = trace_cols - LY + 1
    valid_x = (places < limit_x).astype(jnp.float32)
    counts = (
        counts_along(places, LX, limit_x)[:, None] * counts_along(columns, LY, limit_y)[None, :]
    )
    lag_shift = shift_matrix(trace_cols, LY, limit_y)
    subspace = paired(start_basis)
    next_counts = (
        counts_along(places + strip_width, LX, limit_x)[:, None]
        * counts_along(columns, LY, limit_y)[None, :]
    )[: LX - 1]
    next_counts = jnp.maximum(next_counts, 1.0)
    rim_rows = shifted(slices[:, :, : LX - 1, :], "space", -1)
    for cadzow_step in range(CADZOW):
        extended = jnp.concatenate([slices, rim_rows], axis=2)
        lagged = product("fcpz,zby->fcbpy", extended, lag_shift)
        matrix = jnp.stack(
            [lagged[:, :, :, lag_x : lag_x + strip_width, :] for lag_x in range(LX)], axis=2
        )
        matrix = matrix * valid_x[:, None]
        matrix = matrix.reshape(freq_count, 2 * rows, strip_width * trace_cols)
        gram_h = product("fik,fjk->fij", matrix, matrix, lax.Precision.HIGH)
        cov_real = gram_h[:, :rows, :rows] + gram_h[:, rows:, rows:]
        cov_imag = gram_h[:, rows:, :rows] - gram_h[:, :rows, rows:]
        cov = all_sum(packed(cov_real, cov_imag), "space")
        subspace = power_steps(cov, subspace)
        half = subspace.shape[1] // 2
        signs = jnp.where(jnp.arange(2 * half) < half, 1.0, -1.0)[:, None]
        weights = subspace * signs
        coeffs = product("fjk,fkc->fjc", weights, matrix, lax.Precision.HIGH)
        projected = product("fjk,fjc->fkc", weights, coeffs, lax.Precision.HIGH)
        projected = projected.reshape(freq_count, 2, LX, LY, strip_width, trace_cols)
        along_y = product("fcabxy,vby->fcaxv", projected, lag_shift, lax.Precision.HIGH)
        full = sum(
            jnp.pad(along_y[:, :, lag_x], ((0, 0), (0, 0), (lag_x, LX - 1 - lag_x), (0, 0)))
            for lag_x in range(LX)
        )
        tail = full[:, :, strip_width:, :]
        spill = shifted(tail, "space", 1)
        if cadzow_step + 1 < CADZOW:
            next_head = shifted(full[:, :, : LX - 1, :], "space", -1)
            rim_rows = (next_head + tail) / next_counts
        spill = jnp.pad(spill, ((0, 0), (0, 0), (0, strip_width - (LX - 1)), (0, 0)))
        slices = (full[:, :, :strip_width, :] + spill) / counts
    out_scale = math.sqrt(2.0 / kept_bins.shape[0])
    received = lax.all_to_all(slices, "freq", split_axis=3, concat_axis=0, tiled=True)
    synth = product("fxy,tf->xyt", received[:, 0], cosines)
    synth = synth - product("fxy,tf->xyt", received[:, 1], sines)
    return out_scale * synth


def solution(mesh):
    placed = (P("space", "freq", None), P(), P("freq", None, None, None))
    return jax.shard_map(
        on_device, mesh=mesh, in_specs=placed, out_specs=P("space", "freq", None), check_vma=False
    )
```

```python
import math

import jax
import jax.numpy as jnp
from jax import lax
from jax.experimental import pallas as pl
from jax.experimental.pallas import tpu as pltpu
from jax.sharding import PartitionSpec as P

NT = 2048
LX = 8
LY = 32
RANK = 40
POWER = 4
CADZOW = 2


exact_mode = lax.Precision.HIGHEST


def shifted(x, axis, by):
    count = lax.axis_size(axis)
    pairs = [(i, i + by) for i in range(count) if 0 <= i + by < count]
    return lax.ppermute(x, axis, pairs)


def all_sum(x, axis):
    count = lax.axis_size(axis)
    chunks = x.reshape(count, -1)
    mine = lax.all_to_all(chunks, axis, 0, 0, tiled=True).sum(axis=0)
    copies = jnp.broadcast_to(mine[None], (count, mine.shape[0]))
    return lax.all_to_all(copies, axis, 0, 0, tiled=True).reshape(x.shape)


def product(form, left, right, precision=exact_mode):
    return jnp.einsum(form, left, right, precision=precision, preferred_element_type=jnp.float32)


def tables(kept_bins):
    samples = jnp.arange(NT, dtype=jnp.int32)
    phases = samples[:, None] * kept_bins[None, :] % NT
    angles = phases.astype(jnp.float32) * (2.0 * math.pi / NT)
    return (jnp.cos(angles), jnp.sin(angles))


def paired(start):
    real_rows = jnp.concatenate([start[:, 0], -start[:, 1]], axis=1)
    imag_rows = jnp.concatenate([start[:, 1], start[:, 0]], axis=1)
    return jnp.concatenate([real_rows, imag_rows], axis=2)


def shift_matrix(length, lags, limit):
    shape = (length, lags, length)
    z = lax.broadcasted_iota(jnp.int32, shape, 0)
    b = lax.broadcasted_iota(jnp.int32, shape, 1)
    y = lax.broadcasted_iota(jnp.int32, shape, 2)
    return ((z == y + b) & (y < limit)).astype(jnp.float32)


def realified(real_part, imag_part):
    top = jnp.concatenate([real_part, -imag_part], axis=-1)
    bottom = jnp.concatenate([imag_part, real_part], axis=-1)
    return jnp.concatenate([top, bottom], axis=-2)


def packed(real_part, imag_part):
    upper = lax.broadcasted_iota(jnp.int32, real_part.shape, real_part.ndim - 2) <= lax.broadcasted_iota(
        jnp.int32, real_part.shape, real_part.ndim - 1
    )
    return jnp.where(upper, real_part, imag_part)


def unpacked(square):
    row_id = lax.broadcasted_iota(jnp.int32, square.shape, square.ndim - 2)
    col_id = lax.broadcasted_iota(jnp.int32, square.shape, square.ndim - 1)
    mirrored = jnp.swapaxes(square, -1, -2)
    real_part = jnp.where(row_id <= col_id, square, mirrored)
    imag_part = jnp.where(row_id > col_id, square, jnp.where(row_id == col_id, 0.0, -mirrored))
    return real_part, imag_part


def inverse_factor(left):
    count, width = left.shape
    half = width // 2
    row_id = lax.broadcasted_iota(jnp.int32, left.shape, 0)
    lane_id = lax.broadcasted_iota(jnp.int32, left.shape, 1)
    sign = jnp.where(lane_id[:1] < half, -1.0, 1.0)
    rows_only = row_id[:, :1]

    def body(k, carry):
        left, inverse, pivots = carry
        at_row = row_id == k
        col_real = jnp.sum(jnp.where(lane_id == k, left, 0.0), axis=1, keepdims=True)
        col_imag = jnp.sum(jnp.where(lane_id == k + half, left, 0.0), axis=1, keepdims=True)
        row_left = jnp.sum(jnp.where(at_row, left, 0.0), axis=0, keepdims=True)
        row_inverse = jnp.sum(jnp.where(at_row, inverse, 0.0), axis=0, keepdims=True)
        pivot = jnp.sum(jnp.where(rows_only == k, col_real, 0.0), axis=0, keepdims=True)
        scale = 1.0 / pivot
        below = rows_only > k
        by_real = jnp.where(below, col_real, 0.0) * scale
        by_imag = jnp.where(below, col_imag, 0.0) * scale
        left = left - (by_real * row_left + by_imag * (pltpu.roll(row_left, half, 1) * sign))
        inverse = inverse - (
            by_real * row_inverse + by_imag * (pltpu.roll(row_inverse, half, 1) * sign)
        )
        pivots = jnp.where(rows_only == k, pivot, pivots)
        return left, inverse, pivots

    eye = (row_id == lane_id).astype(jnp.float32)
    start = (left, eye, jnp.zeros((count, 1), jnp.float32))
    _, inverse, pivots = lax.fori_loop(0, count, body, start, unroll=4)
    return inverse * lax.rsqrt(pivots)


def turned(rows):
    width = rows.shape[1] // 2
    return jnp.concatenate([-rows[:, width:], rows[:, :width]], axis=1)


def dot(left, right, precision=exact_mode):
    return jnp.dot(left, right, precision=precision, preferred_element_type=jnp.float32)


def power_kernel(cov_ref, start_ref, out_ref):
    square = cov_ref[0]
    mirrored = square.T
    row_id = lax.broadcasted_iota(jnp.int32, square.shape, 0)
    col_id = lax.broadcasted_iota(jnp.int32, square.shape, 1)
    cov_real = jnp.where(row_id <= col_id, square, mirrored)
    cov_imag = jnp.where(row_id > col_id, square, jnp.where(row_id == col_id, 0.0, -mirrored))
    half = start_ref.shape[1] // 2
    width = square.shape[0]
    subspace = start_ref[0, :half, :]
    pad = jnp.zeros((64 - half, 2 * width), jnp.float32)
    contract = (((1,), (1,)), ((), ()))
    for power_step in range(POWER):
        sub_real = subspace[:, :width]
        sub_imag = subspace[:, width:]
        summed = jnp.concatenate(
            [
                dot(sub_real, cov_real, lax.Precision.HIGH)
                + dot(sub_imag, cov_imag, lax.Precision.HIGH),
                dot(sub_imag, cov_real, lax.Precision.HIGH)
                - dot(sub_real, cov_imag, lax.Precision.HIGH),
            ],
            axis=1,
        )
        stacked = jnp.concatenate([summed, pad, turned(summed), pad], axis=0)
        gram_matrix = lax.dot_general(
            summed, stacked, contract, precision=exact_mode, preferred_element_type=jnp.float32
        )
        subspace = dot(inverse_factor(gram_matrix), stacked)
    out_ref[0, :half, :] = subspace
    out_ref[0, half:, :] = turned(subspace)


def power_steps(cov_square, subspace):
    freq_count, basis, width = subspace.shape
    rows = cov_square.shape[1]
    return pl.pallas_call(
        power_kernel,
        out_shape=jax.ShapeDtypeStruct(subspace.shape, jnp.float32),
        grid=(freq_count,),
        in_specs=[
            pl.BlockSpec((1, rows, rows), lambda i: (i, 0, 0)),
            pl.BlockSpec((1, basis, width), lambda i: (i, 0, 0)),
        ],
        out_specs=pl.BlockSpec((1, basis, width), lambda i: (i, 0, 0)),
    )(cov_square, subspace)


def counts_along(places, lags, limit):
    total = jnp.zeros(places.shape, jnp.float32)
    for shift_by in range(lags):
        inside = (places - shift_by >= 0) & (places - shift_by < limit)
        total = total + inside.astype(jnp.float32)
    return total


def on_device(traces, kept_bins, start_basis):
    space_count = lax.axis_size("space")
    cosines, sines = tables(kept_bins)
    dft_scale = 1.0 / math.sqrt(NT)
    waves = jnp.stack([cosines * dft_scale, -sines * dft_scale], axis=1)
    spectra_tile = product("xyt,tcf->fcxy", traces, waves)
    slices = lax.all_to_all(spectra_tile, "freq", split_axis=0, concat_axis=3, tiled=True)
    freq_count = slices.shape[0]
    strip_width = slices.shape[2]
    trace_cols = slices.shape[3]
    rows = LX * LY
    x_offset = lax.axis_index("space") * strip_width
    places = x_offset + jnp.arange(strip_width, dtype=jnp.int32)
    columns = jnp.arange(trace_cols, dtype=jnp.int32)
    limit_x = strip_width * space_count - LX + 1
    limit_y = trace_cols - LY + 1
    valid_x = (places < limit_x).astype(jnp.float32)
    counts = (
        counts_along(places, LX, limit_x)[:, None] * counts_along(columns, LY, limit_y)[None, :]
    )
    lag_shift = shift_matrix(trace_cols, LY, limit_y)
    subspace = paired(start_basis)
    next_counts = (
        counts_along(places + strip_width, LX, limit_x)[:, None]
        * counts_along(columns, LY, limit_y)[None, :]
    )[: LX - 1]
    next_counts = jnp.maximum(next_counts, 1.0)
    rim_rows = shifted(slices[:, :, : LX - 1, :], "space", -1)
    for cadzow_step in range(CADZOW):
        extended = jnp.concatenate([slices, rim_rows], axis=2)
        lagged = product("fcpz,zby->fcbpy", extended, lag_shift)
        matrix = jnp.stack(
            [lagged[:, :, :, lag_x : lag_x + strip_width, :] for lag_x in range(LX)], axis=2
        )
        matrix = matrix * valid_x[:, None]
        matrix = matrix.reshape(freq_count, 2 * rows, strip_width * trace_cols)
        gram_h = product("fik,fjk->fij", matrix, matrix, lax.Precision.HIGH)
        cov_real = gram_h[:, :rows, :rows] + gram_h[:, rows:, rows:]
        cov_imag = gram_h[:, rows:, :rows] - gram_h[:, :rows, rows:]
        cov = all_sum(packed(cov_real, cov_imag), "space")
        subspace = power_steps(cov, subspace)
        half = subspace.shape[1] // 2
        signs = jnp.where(jnp.arange(2 * half) < half, 1.0, -1.0)[:, None]
        weights = subspace * signs
        coeffs = product("fjk,fkc->fjc", weights, matrix, lax.Precision.HIGH)
        projected = product("fjk,fjc->fkc", weights, coeffs, lax.Precision.HIGH)
        projected = projected.reshape(freq_count, 2, LX, LY, strip_width, trace_cols)
        along_y = product("fcabxy,vby->fcaxv", projected, lag_shift, lax.Precision.HIGH)
        full = sum(
            jnp.pad(along_y[:, :, lag_x], ((0, 0), (0, 0), (lag_x, LX - 1 - lag_x), (0, 0)))
            for lag_x in range(LX)
        )
        tail = full[:, :, strip_width:, :]
        spill = shifted(tail, "space", 1)
        if cadzow_step + 1 < CADZOW:
            next_head = shifted(full[:, :, : LX - 1, :], "space", -1)
            rim_rows = (next_head + tail) / next_counts
        spill = jnp.pad(spill, ((0, 0), (0, 0), (0, strip_width - (LX - 1)), (0, 0)))
        slices = (full[:, :, :strip_width, :] + spill) / counts
    out_scale = math.sqrt(2.0 / kept_bins.shape[0])
    received = lax.all_to_all(slices, "freq", split_axis=3, concat_axis=0, tiled=True)
    synth = product("fxy,tf->xyt", received[:, 0], cosines)
    synth = synth - product("fxy,tf->xyt", received[:, 1], sines)
    return out_scale * synth


def solution(mesh):
    placed = (P("space", "freq", None), P(), P("freq", None, None, None))
    return jax.shard_map(
        on_device, mesh=mesh, in_specs=placed, out_specs=P("space", "freq", None), check_vma=False
    )
```

```python
import math

import jax
import jax.numpy as jnp
from jax import lax
from jax.experimental import pallas as pl
from jax.experimental.pallas import tpu as pltpu
from jax.sharding import PartitionSpec as P

NT = 2048
LX = 8
LY = 32
RANK = 40
POWER = 4
CADZOW = 2


exact_mode = lax.Precision.HIGHEST


def shifted(x, axis, by):
    count = lax.axis_size(axis)
    pairs = [(i, i + by) for i in range(count) if 0 <= i + by < count]
    return lax.ppermute(x, axis, pairs)


def all_sum(x, axis):
    count = lax.axis_size(axis)
    chunks = x.reshape(count, -1)
    mine = lax.all_to_all(chunks, axis, 0, 0, tiled=True).sum(axis=0)
    copies = jnp.broadcast_to(mine[None], (count, mine.shape[0]))
    return lax.all_to_all(copies, axis, 0, 0, tiled=True).reshape(x.shape)


def product(form, left, right, precision=exact_mode):
    return jnp.einsum(form, left, right, precision=precision, preferred_element_type=jnp.float32)


def tables(kept_bins):
    samples = jnp.arange(NT, dtype=jnp.int32)
    phases = samples[:, None] * kept_bins[None, :] % NT
    angles = phases.astype(jnp.float32) * (2.0 * math.pi / NT)
    return (jnp.cos(angles), jnp.sin(angles))


def paired(start):
    real_rows = jnp.concatenate([start[:, 0], -start[:, 1]], axis=1)
    imag_rows = jnp.concatenate([start[:, 1], start[:, 0]], axis=1)
    return jnp.concatenate([real_rows, imag_rows], axis=2)


def shift_matrix(length, lags, limit):
    shape = (length, lags, length)
    z = lax.broadcasted_iota(jnp.int32, shape, 0)
    b = lax.broadcasted_iota(jnp.int32, shape, 1)
    y = lax.broadcasted_iota(jnp.int32, shape, 2)
    return ((z == y + b) & (y < limit)).astype(jnp.float32)


def realified(real_part, imag_part):
    top = jnp.concatenate([real_part, -imag_part], axis=-1)
    bottom = jnp.concatenate([imag_part, real_part], axis=-1)
    return jnp.concatenate([top, bottom], axis=-2)


def packed(real_part, imag_part):
    upper = lax.broadcasted_iota(jnp.int32, real_part.shape, real_part.ndim - 2) <= lax.broadcasted_iota(
        jnp.int32, real_part.shape, real_part.ndim - 1
    )
    return jnp.where(upper, real_part, imag_part)


def unpacked(square):
    row_id = lax.broadcasted_iota(jnp.int32, square.shape, square.ndim - 2)
    col_id = lax.broadcasted_iota(jnp.int32, square.shape, square.ndim - 1)
    mirrored = jnp.swapaxes(square, -1, -2)
    real_part = jnp.where(row_id <= col_id, square, mirrored)
    imag_part = jnp.where(row_id > col_id, square, jnp.where(row_id == col_id, 0.0, -mirrored))
    return real_part, imag_part


def inverse_factor(left):
    count, width = left.shape
    half = width // 2
    row_id = lax.broadcasted_iota(jnp.int32, left.shape, 0)
    lane_id = lax.broadcasted_iota(jnp.int32, left.shape, 1)
    sign = jnp.where(lane_id[:1] < half, -1.0, 1.0)
    rows_only = row_id[:, :1]

    def body(k, carry):
        left, inverse, pivots = carry
        at_row = row_id == k
        col_real = jnp.sum(jnp.where(lane_id == k, left, 0.0), axis=1, keepdims=True)
        col_imag = jnp.sum(jnp.where(lane_id == k + half, left, 0.0), axis=1, keepdims=True)
        row_left = jnp.sum(jnp.where(at_row, left, 0.0), axis=0, keepdims=True)
        row_inverse = jnp.sum(jnp.where(at_row, inverse, 0.0), axis=0, keepdims=True)
        pivot = jnp.sum(jnp.where(rows_only == k, col_real, 0.0), axis=0, keepdims=True)
        scale = 1.0 / pivot
        below = rows_only > k
        by_real = jnp.where(below, col_real, 0.0) * scale
        by_imag = jnp.where(below, col_imag, 0.0) * scale
        left = left - (by_real * row_left + by_imag * (pltpu.roll(row_left, half, 1) * sign))
        inverse = inverse - (
            by_real * row_inverse + by_imag * (pltpu.roll(row_inverse, half, 1) * sign)
        )
        pivots = jnp.where(rows_only == k, pivot, pivots)
        return left, inverse, pivots

    eye = (row_id == lane_id).astype(jnp.float32)
    start = (left, eye, jnp.zeros((count, 1), jnp.float32))
    _, inverse, pivots = lax.fori_loop(0, count, body, start, unroll=4)
    return inverse * lax.rsqrt(pivots)


def turned(rows):
    width = rows.shape[1] // 2
    return jnp.concatenate([-rows[:, width:], rows[:, :width]], axis=1)


def dot(left, right, precision=exact_mode):
    return jnp.dot(left, right, precision=precision, preferred_element_type=jnp.float32)


def power_kernel(cov_ref, start_ref, out_ref):
    square = cov_ref[0]
    mirrored = square.T
    row_id = lax.broadcasted_iota(jnp.int32, square.shape, 0)
    col_id = lax.broadcasted_iota(jnp.int32, square.shape, 1)
    cov_real = jnp.where(row_id <= col_id, square, mirrored)
    cov_imag = jnp.where(row_id > col_id, square, jnp.where(row_id == col_id, 0.0, -mirrored))
    half = start_ref.shape[1] // 2
    width = square.shape[0]
    subspace = start_ref[0, :half, :]
    pad = jnp.zeros((64 - half, 2 * width), jnp.float32)
    contract = (((1,), (1,)), ((), ()))
    for power_step in range(POWER):
        sub_real = subspace[:, :width]
        sub_imag = subspace[:, width:]
        summed = jnp.concatenate(
            [
                dot(sub_real, cov_real, lax.Precision.HIGH)
                + dot(sub_imag, cov_imag, lax.Precision.HIGH),
                dot(sub_imag, cov_real, lax.Precision.HIGH)
                - dot(sub_real, cov_imag, lax.Precision.HIGH),
            ],
            axis=1,
        )
        stacked = jnp.concatenate([summed, pad, turned(summed), pad], axis=0)
        gram_matrix = lax.dot_general(
            summed, stacked, contract, precision=exact_mode, preferred_element_type=jnp.float32
        )
        subspace = dot(inverse_factor(gram_matrix), stacked)
    out_ref[0, :half, :] = subspace
    out_ref[0, half:, :] = turned(subspace)


def power_steps(cov_square, subspace):
    freq_count, basis, width = subspace.shape
    rows = cov_square.shape[1]
    return pl.pallas_call(
        power_kernel,
        out_shape=jax.ShapeDtypeStruct(subspace.shape, jnp.float32),
        grid=(freq_count,),
        in_specs=[
            pl.BlockSpec((1, rows, rows), lambda i: (i, 0, 0)),
            pl.BlockSpec((1, basis, width), lambda i: (i, 0, 0)),
        ],
        out_specs=pl.BlockSpec((1, basis, width), lambda i: (i, 0, 0)),
    )(cov_square, subspace)


def counts_along(places, lags, limit):
    total = jnp.zeros(places.shape, jnp.float32)
    for shift_by in range(lags):
        inside = (places - shift_by >= 0) & (places - shift_by < limit)
        total = total + inside.astype(jnp.float32)
    return total


def on_device(traces, kept_bins, start_basis):
    space_count = lax.axis_size("space")
    cosines, sines = tables(kept_bins)
    dft_scale = 1.0 / math.sqrt(NT)
    waves = jnp.stack([cosines * dft_scale, -sines * dft_scale], axis=1)
    spectra_tile = product("xyt,tcf->fcxy", traces, waves, lax.Precision.HIGH)
    slices = lax.all_to_all(spectra_tile, "freq", split_axis=0, concat_axis=3, tiled=True)
    freq_count = slices.shape[0]
    strip_width = slices.shape[2]
    trace_cols = slices.shape[3]
    rows = LX * LY
    x_offset = lax.axis_index("space") * strip_width
    places = x_offset + jnp.arange(strip_width, dtype=jnp.int32)
    columns = jnp.arange(trace_cols, dtype=jnp.int32)
    limit_x = strip_width * space_count - LX + 1
    limit_y = trace_cols - LY + 1
    valid_x = (places < limit_x).astype(jnp.float32)
    counts = (
        counts_along(places, LX, limit_x)[:, None] * counts_along(columns, LY, limit_y)[None, :]
    )
    lag_shift = shift_matrix(trace_cols, LY, limit_y)
    subspace = paired(start_basis)
    next_counts = (
        counts_along(places + strip_width, LX, limit_x)[:, None]
        * counts_along(columns, LY, limit_y)[None, :]
    )[: LX - 1]
    next_counts = jnp.maximum(next_counts, 1.0)
    rim_rows = shifted(slices[:, :, : LX - 1, :], "space", -1)
    for cadzow_step in range(CADZOW):
        extended = jnp.concatenate([slices, rim_rows], axis=2)
        lagged = product("fcpz,zby->fcbpy", extended, lag_shift)
        matrix = jnp.stack(
            [lagged[:, :, :, lag_x : lag_x + strip_width, :] for lag_x in range(LX)], axis=2
        )
        matrix = matrix * valid_x[:, None]
        matrix = matrix.reshape(freq_count, 2 * rows, strip_width * trace_cols)
        gram_h = product("fik,fjk->fij", matrix, matrix, lax.Precision.HIGH)
        cov_real = gram_h[:, :rows, :rows] + gram_h[:, rows:, rows:]
        cov_imag = gram_h[:, rows:, :rows] - gram_h[:, :rows, rows:]
        cov = all_sum(packed(cov_real, cov_imag), "space")
        subspace = power_steps(cov, subspace)
        half = subspace.shape[1] // 2
        signs = jnp.where(jnp.arange(2 * half) < half, 1.0, -1.0)[:, None]
        weights = subspace * signs
        coeffs = product("fjk,fkc->fjc", weights, matrix, lax.Precision.HIGH)
        projected = product("fjk,fjc->fkc", weights, coeffs, lax.Precision.HIGH)
        projected = projected.reshape(freq_count, 2, LX, LY, strip_width, trace_cols)
        along_y = product("fcabxy,vby->fcaxv", projected, lag_shift, lax.Precision.HIGH)
        full = sum(
            jnp.pad(along_y[:, :, lag_x], ((0, 0), (0, 0), (lag_x, LX - 1 - lag_x), (0, 0)))
            for lag_x in range(LX)
        )
        tail = full[:, :, strip_width:, :]
        spill = shifted(tail, "space", 1)
        if cadzow_step + 1 < CADZOW:
            next_head = shifted(full[:, :, : LX - 1, :], "space", -1)
            rim_rows = (next_head + tail) / next_counts
        spill = jnp.pad(spill, ((0, 0), (0, 0), (0, strip_width - (LX - 1)), (0, 0)))
        slices = (full[:, :, :strip_width, :] + spill) / counts
    out_scale = math.sqrt(2.0 / kept_bins.shape[0])
    received = lax.all_to_all(slices, "freq", split_axis=3, concat_axis=0, tiled=True)
    synth = product("fxy,tf->xyt", received[:, 0], cosines)
    synth = synth - product("fxy,tf->xyt", received[:, 1], sines)
    return out_scale * synth


def solution(mesh):
    placed = (P("space", "freq", None), P(), P("freq", None, None, None))
    return jax.shard_map(
        on_device, mesh=mesh, in_specs=placed, out_specs=P("space", "freq", None), check_vma=False
    )
```

```python
import math

import jax
import jax.numpy as jnp
from jax import lax
from jax.experimental import pallas as pl
from jax.experimental.pallas import tpu as pltpu
from jax.sharding import PartitionSpec as P

NT = 2048
LX = 8
LY = 32
RANK = 40
POWER = 4
CADZOW = 2


exact_mode = lax.Precision.HIGHEST


def shifted(x, axis, by):
    count = lax.axis_size(axis)
    pairs = [(i, i + by) for i in range(count) if 0 <= i + by < count]
    return lax.ppermute(x, axis, pairs)


def all_sum(x, axis):
    count = lax.axis_size(axis)
    chunks = x.reshape(count, -1)
    mine = lax.all_to_all(chunks, axis, 0, 0, tiled=True).sum(axis=0)
    copies = jnp.broadcast_to(mine[None], (count, mine.shape[0]))
    return lax.all_to_all(copies, axis, 0, 0, tiled=True).reshape(x.shape)


def product(form, left, right, precision=exact_mode):
    return jnp.einsum(form, left, right, precision=precision, preferred_element_type=jnp.float32)


def tables(kept_bins):
    samples = jnp.arange(NT, dtype=jnp.int32)
    phases = samples[:, None] * kept_bins[None, :] % NT
    angles = phases.astype(jnp.float32) * (2.0 * math.pi / NT)
    return (jnp.cos(angles), jnp.sin(angles))


def paired(start):
    real_rows = jnp.concatenate([start[:, 0], -start[:, 1]], axis=1)
    imag_rows = jnp.concatenate([start[:, 1], start[:, 0]], axis=1)
    return jnp.concatenate([real_rows, imag_rows], axis=2)


def shift_matrix(length, lags, limit):
    shape = (length, lags, length)
    z = lax.broadcasted_iota(jnp.int32, shape, 0)
    b = lax.broadcasted_iota(jnp.int32, shape, 1)
    y = lax.broadcasted_iota(jnp.int32, shape, 2)
    return ((z == y + b) & (y < limit)).astype(jnp.float32)


def realified(real_part, imag_part):
    top = jnp.concatenate([real_part, -imag_part], axis=-1)
    bottom = jnp.concatenate([imag_part, real_part], axis=-1)
    return jnp.concatenate([top, bottom], axis=-2)


def packed(real_part, imag_part):
    upper = lax.broadcasted_iota(jnp.int32, real_part.shape, real_part.ndim - 2) <= lax.broadcasted_iota(
        jnp.int32, real_part.shape, real_part.ndim - 1
    )
    return jnp.where(upper, real_part, imag_part)


def unpacked(square):
    row_id = lax.broadcasted_iota(jnp.int32, square.shape, square.ndim - 2)
    col_id = lax.broadcasted_iota(jnp.int32, square.shape, square.ndim - 1)
    mirrored = jnp.swapaxes(square, -1, -2)
    real_part = jnp.where(row_id <= col_id, square, mirrored)
    imag_part = jnp.where(row_id > col_id, square, jnp.where(row_id == col_id, 0.0, -mirrored))
    return real_part, imag_part


def inverse_factor(left):
    count, width = left.shape
    half = width // 2
    row_id = lax.broadcasted_iota(jnp.int32, left.shape, 0)
    lane_id = lax.broadcasted_iota(jnp.int32, left.shape, 1)
    sign = jnp.where(lane_id[:1] < half, -1.0, 1.0)
    rows_only = row_id[:, :1]

    def body(k, carry):
        left, inverse, pivots = carry
        at_row = row_id == k
        col_real = jnp.sum(jnp.where(lane_id == k, left, 0.0), axis=1, keepdims=True)
        col_imag = jnp.sum(jnp.where(lane_id == k + half, left, 0.0), axis=1, keepdims=True)
        row_left = jnp.sum(jnp.where(at_row, left, 0.0), axis=0, keepdims=True)
        row_inverse = jnp.sum(jnp.where(at_row, inverse, 0.0), axis=0, keepdims=True)
        pivot = jnp.sum(jnp.where(rows_only == k, col_real, 0.0), axis=0, keepdims=True)
        scale = 1.0 / pivot
        below = rows_only > k
        by_real = jnp.where(below, col_real, 0.0) * scale
        by_imag = jnp.where(below, col_imag, 0.0) * scale
        left = left - (by_real * row_left + by_imag * (pltpu.roll(row_left, half, 1) * sign))
        inverse = inverse - (
            by_real * row_inverse + by_imag * (pltpu.roll(row_inverse, half, 1) * sign)
        )
        pivots = jnp.where(rows_only == k, pivot, pivots)
        return left, inverse, pivots

    eye = (row_id == lane_id).astype(jnp.float32)
    start = (left, eye, jnp.zeros((count, 1), jnp.float32))
    _, inverse, pivots = lax.fori_loop(0, count, body, start, unroll=4)
    return inverse * lax.rsqrt(pivots)


def turned(rows):
    width = rows.shape[1] // 2
    return jnp.concatenate([-rows[:, width:], rows[:, :width]], axis=1)


def dot(left, right, precision=exact_mode):
    return jnp.dot(left, right, precision=precision, preferred_element_type=jnp.float32)


def power_kernel(cov_ref, start_ref, out_ref):
    square = cov_ref[0]
    mirrored = square.T
    row_id = lax.broadcasted_iota(jnp.int32, square.shape, 0)
    col_id = lax.broadcasted_iota(jnp.int32, square.shape, 1)
    cov_real = jnp.where(row_id <= col_id, square, mirrored)
    cov_imag = jnp.where(row_id > col_id, square, jnp.where(row_id == col_id, 0.0, -mirrored))
    half = start_ref.shape[1] // 2
    width = square.shape[0]
    subspace = start_ref[0, :half, :]
    pad = jnp.zeros((64 - half, 2 * width), jnp.float32)
    contract = (((1,), (1,)), ((), ()))
    for power_step in range(POWER):
        sub_real = subspace[:, :width]
        sub_imag = subspace[:, width:]
        summed = jnp.concatenate(
            [
                dot(sub_real, cov_real, lax.Precision.HIGH)
                + dot(sub_imag, cov_imag, lax.Precision.HIGH),
                dot(sub_imag, cov_real, lax.Precision.HIGH)
                - dot(sub_real, cov_imag, lax.Precision.HIGH),
            ],
            axis=1,
        )
        stacked = jnp.concatenate([summed, pad, turned(summed), pad], axis=0)
        gram_matrix = lax.dot_general(
            summed, stacked, contract, precision=exact_mode, preferred_element_type=jnp.float32
        )
        subspace = dot(inverse_factor(gram_matrix), stacked)
    out_ref[0, :half, :] = subspace
    out_ref[0, half:, :] = turned(subspace)


def power_steps(cov_square, subspace):
    freq_count, basis, width = subspace.shape
    rows = cov_square.shape[1]
    return pl.pallas_call(
        power_kernel,
        out_shape=jax.ShapeDtypeStruct(subspace.shape, jnp.float32),
        grid=(freq_count,),
        in_specs=[
            pl.BlockSpec((1, rows, rows), lambda i: (i, 0, 0)),
            pl.BlockSpec((1, basis, width), lambda i: (i, 0, 0)),
        ],
        out_specs=pl.BlockSpec((1, basis, width), lambda i: (i, 0, 0)),
    )(cov_square, subspace)


def counts_along(places, lags, limit):
    total = jnp.zeros(places.shape, jnp.float32)
    for shift_by in range(lags):
        inside = (places - shift_by >= 0) & (places - shift_by < limit)
        total = total + inside.astype(jnp.float32)
    return total


def on_device(traces, kept_bins, start_basis):
    space_count = lax.axis_size("space")
    cosines, sines = tables(kept_bins)
    dft_scale = 1.0 / math.sqrt(NT)
    waves = jnp.stack([cosines * dft_scale, -sines * dft_scale], axis=1)
    spectra_tile = product("xyt,tcf->fcxy", traces, waves)
    slices = lax.all_to_all(spectra_tile, "freq", split_axis=0, concat_axis=3, tiled=True)
    freq_count = slices.shape[0]
    strip_width = slices.shape[2]
    trace_cols = slices.shape[3]
    rows = LX * LY
    x_offset = lax.axis_index("space") * strip_width
    places = x_offset + jnp.arange(strip_width, dtype=jnp.int32)
    columns = jnp.arange(trace_cols, dtype=jnp.int32)
    limit_x = strip_width * space_count - LX + 1
    limit_y = trace_cols - LY + 1
    valid_x = (places < limit_x).astype(jnp.float32)
    counts = (
        counts_along(places, LX, limit_x)[:, None] * counts_along(columns, LY, limit_y)[None, :]
    )
    lag_shift = shift_matrix(trace_cols, LY, limit_y)
    subspace = paired(start_basis)
    next_counts = (
        counts_along(places + strip_width, LX, limit_x)[:, None]
        * counts_along(columns, LY, limit_y)[None, :]
    )[: LX - 1]
    next_counts = jnp.maximum(next_counts, 1.0)
    rim_rows = shifted(slices[:, :, : LX - 1, :], "space", -1)
    for cadzow_step in range(CADZOW):
        extended = jnp.concatenate([slices, rim_rows], axis=2)
        lagged = product("fcpz,zby->fcbpy", extended, lag_shift, lax.Precision.HIGH)
        matrix = jnp.stack(
            [lagged[:, :, :, lag_x : lag_x + strip_width, :] for lag_x in range(LX)], axis=2
        )
        matrix = matrix * valid_x[:, None]
        matrix = matrix.reshape(freq_count, 2 * rows, strip_width * trace_cols)
        gram_h = product("fik,fjk->fij", matrix, matrix, lax.Precision.HIGH)
        cov_real = gram_h[:, :rows, :rows] + gram_h[:, rows:, rows:]
        cov_imag = gram_h[:, rows:, :rows] - gram_h[:, :rows, rows:]
        cov = all_sum(packed(cov_real, cov_imag), "space")
        subspace = power_steps(cov, subspace)
        half = subspace.shape[1] // 2
        signs = jnp.where(jnp.arange(2 * half) < half, 1.0, -1.0)[:, None]
        weights = subspace * signs
        coeffs = product("fjk,fkc->fjc", weights, matrix, lax.Precision.HIGH)
        projected = product("fjk,fjc->fkc", weights, coeffs, lax.Precision.HIGH)
        projected = projected.reshape(freq_count, 2, LX, LY, strip_width, trace_cols)
        along_y = product("fcabxy,vby->fcaxv", projected, lag_shift, lax.Precision.HIGH)
        full = sum(
            jnp.pad(along_y[:, :, lag_x], ((0, 0), (0, 0), (lag_x, LX - 1 - lag_x), (0, 0)))
            for lag_x in range(LX)
        )
        tail = full[:, :, strip_width:, :]
        spill = shifted(tail, "space", 1)
        if cadzow_step + 1 < CADZOW:
            next_head = shifted(full[:, :, : LX - 1, :], "space", -1)
            rim_rows = (next_head + tail) / next_counts
        spill = jnp.pad(spill, ((0, 0), (0, 0), (0, strip_width - (LX - 1)), (0, 0)))
        slices = (full[:, :, :strip_width, :] + spill) / counts
    out_scale = math.sqrt(2.0 / kept_bins.shape[0])
    received = lax.all_to_all(slices, "freq", split_axis=3, concat_axis=0, tiled=True)
    synth = product("fxy,tf->xyt", received[:, 0], cosines)
    synth = synth - product("fxy,tf->xyt", received[:, 1], sines)
    return out_scale * synth


def solution(mesh):
    placed = (P("space", "freq", None), P(), P("freq", None, None, None))
    return jax.shard_map(
        on_device, mesh=mesh, in_specs=placed, out_specs=P("space", "freq", None), check_vma=False
    )
```

```python
import math

import jax
import jax.numpy as jnp
from jax import lax
from jax.experimental import pallas as pl
from jax.experimental.pallas import tpu as pltpu
from jax.sharding import PartitionSpec as P

NT = 2048
LX = 8
LY = 32
RANK = 40
POWER = 4
CADZOW = 2


exact_mode = lax.Precision.HIGHEST


def shifted(x, axis, by):
    count = lax.axis_size(axis)
    pairs = [(i, i + by) for i in range(count) if 0 <= i + by < count]
    return lax.ppermute(x, axis, pairs)


def all_sum(x, axis):
    count = lax.axis_size(axis)
    chunks = x.reshape(count, -1)
    mine = lax.all_to_all(chunks, axis, 0, 0, tiled=True).sum(axis=0)
    copies = jnp.broadcast_to(mine[None], (count, mine.shape[0]))
    return lax.all_to_all(copies, axis, 0, 0, tiled=True).reshape(x.shape)


def product(form, left, right, precision=exact_mode):
    return jnp.einsum(form, left, right, precision=precision, preferred_element_type=jnp.float32)


def tables(kept_bins):
    samples = jnp.arange(NT, dtype=jnp.int32)
    phases = samples[:, None] * kept_bins[None, :] % NT
    angles = phases.astype(jnp.float32) * (2.0 * math.pi / NT)
    return (jnp.cos(angles), jnp.sin(angles))


def paired(start):
    real_rows = jnp.concatenate([start[:, 0], -start[:, 1]], axis=1)
    imag_rows = jnp.concatenate([start[:, 1], start[:, 0]], axis=1)
    return jnp.concatenate([real_rows, imag_rows], axis=2)


def shift_matrix(length, lags, limit):
    shape = (length, lags, length)
    z = lax.broadcasted_iota(jnp.int32, shape, 0)
    b = lax.broadcasted_iota(jnp.int32, shape, 1)
    y = lax.broadcasted_iota(jnp.int32, shape, 2)
    return ((z == y + b) & (y < limit)).astype(jnp.float32)


def realified(real_part, imag_part):
    top = jnp.concatenate([real_part, -imag_part], axis=-1)
    bottom = jnp.concatenate([imag_part, real_part], axis=-1)
    return jnp.concatenate([top, bottom], axis=-2)


def packed(real_part, imag_part):
    upper = lax.broadcasted_iota(jnp.int32, real_part.shape, real_part.ndim - 2) <= lax.broadcasted_iota(
        jnp.int32, real_part.shape, real_part.ndim - 1
    )
    return jnp.where(upper, real_part, imag_part)


def unpacked(square):
    row_id = lax.broadcasted_iota(jnp.int32, square.shape, square.ndim - 2)
    col_id = lax.broadcasted_iota(jnp.int32, square.shape, square.ndim - 1)
    mirrored = jnp.swapaxes(square, -1, -2)
    real_part = jnp.where(row_id <= col_id, square, mirrored)
    imag_part = jnp.where(row_id > col_id, square, jnp.where(row_id == col_id, 0.0, -mirrored))
    return real_part, imag_part


def inverse_factor(left):
    count, width = left.shape
    half = width // 2
    row_id = lax.broadcasted_iota(jnp.int32, left.shape, 0)
    lane_id = lax.broadcasted_iota(jnp.int32, left.shape, 1)
    sign = jnp.where(lane_id[:1] < half, -1.0, 1.0)
    rows_only = row_id[:, :1]

    def body(k, carry):
        left, inverse, pivots = carry
        at_row = row_id == k
        col_real = jnp.sum(jnp.where(lane_id == k, left, 0.0), axis=1, keepdims=True)
        col_imag = jnp.sum(jnp.where(lane_id == k + half, left, 0.0), axis=1, keepdims=True)
        row_left = jnp.sum(jnp.where(at_row, left, 0.0), axis=0, keepdims=True)
        row_inverse = jnp.sum(jnp.where(at_row, inverse, 0.0), axis=0, keepdims=True)
        pivot = jnp.sum(jnp.where(rows_only == k, col_real, 0.0), axis=0, keepdims=True)
        scale = 1.0 / pivot
        below = rows_only > k
        by_real = jnp.where(below, col_real, 0.0) * scale
        by_imag = jnp.where(below, col_imag, 0.0) * scale
        left = left - (by_real * row_left + by_imag * (pltpu.roll(row_left, half, 1) * sign))
        inverse = inverse - (
            by_real * row_inverse + by_imag * (pltpu.roll(row_inverse, half, 1) * sign)
        )
        pivots = jnp.where(rows_only == k, pivot, pivots)
        return left, inverse, pivots

    eye = (row_id == lane_id).astype(jnp.float32)
    start = (left, eye, jnp.zeros((count, 1), jnp.float32))
    _, inverse, pivots = lax.fori_loop(0, count, body, start, unroll=4)
    return inverse * lax.rsqrt(pivots)


def turned(rows):
    width = rows.shape[1] // 2
    return jnp.concatenate([-rows[:, width:], rows[:, :width]], axis=1)


def dot(left, right, precision=exact_mode):
    return jnp.dot(left, right, precision=precision, preferred_element_type=jnp.float32)


def power_kernel(cov_ref, start_ref, out_ref):
    square = cov_ref[0]
    mirrored = square.T
    row_id = lax.broadcasted_iota(jnp.int32, square.shape, 0)
    col_id = lax.broadcasted_iota(jnp.int32, square.shape, 1)
    cov_real = jnp.where(row_id <= col_id, square, mirrored)
    cov_imag = jnp.where(row_id > col_id, square, jnp.where(row_id == col_id, 0.0, -mirrored))
    half = start_ref.shape[1] // 2
    width = square.shape[0]
    subspace = start_ref[0, :half, :]
    pad = jnp.zeros((64 - half, 2 * width), jnp.float32)
    contract = (((1,), (1,)), ((), ()))
    for power_step in range(POWER):
        sub_real = subspace[:, :width]
        sub_imag = subspace[:, width:]
        summed = jnp.concatenate(
            [
                dot(sub_real, cov_real, lax.Precision.HIGH)
                + dot(sub_imag, cov_imag, lax.Precision.HIGH),
                dot(sub_imag, cov_real, lax.Precision.HIGH)
                - dot(sub_real, cov_imag, lax.Precision.HIGH),
            ],
            axis=1,
        )
        stacked = jnp.concatenate([summed, pad, turned(summed), pad], axis=0)
        gram_matrix = lax.dot_general(
            summed, stacked, contract, precision=exact_mode, preferred_element_type=jnp.float32
        )
        subspace = dot(inverse_factor(gram_matrix), stacked)
    out_ref[0, :half, :] = subspace
    out_ref[0, half:, :] = turned(subspace)


def power_steps(cov_square, subspace):
    freq_count, basis, width = subspace.shape
    rows = cov_square.shape[1]
    return pl.pallas_call(
        power_kernel,
        out_shape=jax.ShapeDtypeStruct(subspace.shape, jnp.float32),
        grid=(freq_count,),
        in_specs=[
            pl.BlockSpec((1, rows, rows), lambda i: (i, 0, 0)),
            pl.BlockSpec((1, basis, width), lambda i: (i, 0, 0)),
        ],
        out_specs=pl.BlockSpec((1, basis, width), lambda i: (i, 0, 0)),
    )(cov_square, subspace)


def counts_along(places, lags, limit):
    total = jnp.zeros(places.shape, jnp.float32)
    for shift_by in range(lags):
        inside = (places - shift_by >= 0) & (places - shift_by < limit)
        total = total + inside.astype(jnp.float32)
    return total


def on_device(traces, kept_bins, start_basis):
    space_count = lax.axis_size("space")
    cosines, sines = tables(kept_bins)
    dft_scale = 1.0 / math.sqrt(NT)
    waves = jnp.stack([cosines * dft_scale, -sines * dft_scale], axis=1)
    spectra_tile = product("xyt,tcf->fcxy", traces, waves)
    slices = lax.all_to_all(spectra_tile, "freq", split_axis=0, concat_axis=3, tiled=True)
    freq_count = slices.shape[0]
    strip_width = slices.shape[2]
    trace_cols = slices.shape[3]
    rows = LX * LY
    x_offset = lax.axis_index("space") * strip_width
    places = x_offset + jnp.arange(strip_width, dtype=jnp.int32)
    columns = jnp.arange(trace_cols, dtype=jnp.int32)
    limit_x = strip_width * space_count - LX + 1
    limit_y = trace_cols - LY + 1
    valid_x = (places < limit_x).astype(jnp.float32)
    counts = (
        counts_along(places, LX, limit_x)[:, None] * counts_along(columns, LY, limit_y)[None, :]
    )
    lag_shift = shift_matrix(trace_cols, LY, limit_y)
    subspace = paired(start_basis)
    next_counts = (
        counts_along(places + strip_width, LX, limit_x)[:, None]
        * counts_along(columns, LY, limit_y)[None, :]
    )[: LX - 1]
    next_counts = jnp.maximum(next_counts, 1.0)
    rim_rows = shifted(slices[:, :, : LX - 1, :], "space", -1)
    for cadzow_step in range(CADZOW):
        extended = jnp.concatenate([slices, rim_rows], axis=2)
        lagged = product("fcpz,zby->fcbpy", extended, lag_shift)
        matrix = jnp.stack(
            [lagged[:, :, :, lag_x : lag_x + strip_width, :] for lag_x in range(LX)], axis=2
        )
        matrix = matrix * valid_x[:, None]
        matrix = matrix.reshape(freq_count, 2 * rows, strip_width * trace_cols)
        gram_h = product("fik,fjk->fij", matrix, matrix, lax.Precision.HIGH)
        cov_real = gram_h[:, :rows, :rows] + gram_h[:, rows:, rows:]
        cov_imag = gram_h[:, rows:, :rows] - gram_h[:, :rows, rows:]
        cov = all_sum(packed(cov_real, cov_imag), "space")
        subspace = power_steps(cov, subspace)
        half = subspace.shape[1] // 2
        signs = jnp.where(jnp.arange(2 * half) < half, 1.0, -1.0)[:, None]
        weights = subspace * signs
        coeffs = product("fjk,fkc->fjc", weights, matrix, lax.Precision.HIGH)
        projected = product("fjk,fjc->fkc", weights, coeffs, lax.Precision.HIGH)
        projected = projected.reshape(freq_count, 2, LX, LY, strip_width, trace_cols)
        along_y = product("fcabxy,vby->fcaxv", projected, lag_shift, lax.Precision.HIGH)
        full = sum(
            jnp.pad(along_y[:, :, lag_x], ((0, 0), (0, 0), (lag_x, LX - 1 - lag_x), (0, 0)))
            for lag_x in range(LX)
        )
        tail = full[:, :, strip_width:, :]
        spill = shifted(tail, "space", 1)
        if cadzow_step + 1 < CADZOW:
            next_head = shifted(full[:, :, : LX - 1, :], "space", -1)
            rim_rows = (next_head + tail) / next_counts
        spill = jnp.pad(spill, ((0, 0), (0, 0), (0, strip_width - (LX - 1)), (0, 0)))
        slices = (full[:, :, :strip_width, :] + spill) / counts
    out_scale = math.sqrt(2.0 / kept_bins.shape[0])
    received = lax.all_to_all(slices, "freq", split_axis=3, concat_axis=0, tiled=True)
    synth = product("fxy,tf->xyt", received[:, 0], cosines, lax.Precision.HIGH)
    synth = synth - product("fxy,tf->xyt", received[:, 1], sines, lax.Precision.HIGH)
    return out_scale * synth


def solution(mesh):
    placed = (P("space", "freq", None), P(), P("freq", None, None, None))
    return jax.shard_map(
        on_device, mesh=mesh, in_specs=placed, out_specs=P("space", "freq", None), check_vma=False
    )
```
